32 devices in a mesh: dp: 8 (over y, x, core), tensor: 4 (over z).
Axes of the slice: x: 2, y: 2, z: 4, core: 2. Of those that a mesh axis runs over, the one named last changes fastest.
Arguments:
- inputs: float32 [4096, 768], P(('dp', 'tensor')), may hold values from -6 to 6
- lengths: int32 [8], P('dp'), may hold values from 64 to 512, as said below
- qkv_weight: bfloat16 [1, 3, 768, 768], P(None, None, 'dp', 'tensor'), may hold values from -0.21875 to 0.21875
- qv_bias: float32 [1, 2, 768], P(None, None, 'tensor'), may hold values from -3 to 3
- proj_weight: bfloat16 [1, 768, 768], P(None, 'tensor', 'dp'), may hold values from -1.75 to 1.75
- branch_bias: float32 [1, 2, 768], replicated, may hold values from -3 to 3
- up_weight: bfloat16 [1, 768, 3072], P(None, 'dp', 'tensor'), may hold values from -0.21875 to 0.21875
- up_bias: float32 [1, 3072], P(None, 'tensor'), may hold values from -3 to 3
- down_weight: bfloat16 [1, 3072, 768], P(None, 'tensor', 'dp'), may hold values from -0.109375 to 0.109375
- norm_gain: float32 [1, 2, 768], replicated, may hold values from 0.5 to 1.5
- norm_bias: float32 [1, 2, 768], replicated, may hold values from -3 to 3
- cotangent: float32 [4096, 768], P(('dp', 'tensor')), may hold values from -6 to 6
Outputs:
- outputs: float32 [4096, 768], P(('dp', 'tensor'))
- input_grad: float32 [4096, 768], P(('dp', 'tensor'))
- qkv_grad: float32 [1, 3, 768, 768], P(None, None, 'dp', 'tensor')
- qvbias_grad: float32 [1, 2, 768], P(None, None, 'tensor')
- proj_grad: float32 [1, 768, 768], P(None, 'tensor', 'dp')
- branch_grad: float32 [1, 2, 768], replicated
- up_grad: float32 [1, 768, 3072], P(None, 'dp', 'tensor')
- upbias_grad: float32 [1, 3072], P(None, 'tensor')
- down_grad: float32 [1, 3072, 768], P(None, 'tensor', 'dp')
- gain_grad: float32 [1, 2, 768], replicated
- normbias_grad: float32 [1, 2, 768], replicated
The draws below stay inside these ranges and needn't reach their ends.
Inputs may be any that keep to these rules, and one draw needn't show every extreme that they name: `lengths`: every draw has a sequence with all 512 tokens valid.
All inputs are finite; a program needn't handle non-finite values.
Results may differ from the reference program's by a relative error of at most 0.019.
Values may be sent and summed in bfloat16 or wider, within the bound.
A program may use at most 64 MiB of HBM per device.

```python
import math
import jax
import jax.numpy as jnp
from jax import lax

D = 768
HEADS = 12
HD = 64
FF = 3072
L = 512
LAYERS = 1
SEQS = 8
TOKENS = 4096


def draw_lengths(key, part):
    key_one, key_two = jax.random.split(key)
    drawn = jax.random.randint(key_one, (SEQS,), L // 8, L + 1)
    chosen = jax.random.randint(key_two, (), 0, SEQS)
    return jnp.where(jnp.arange(SEQS) == chosen, L, drawn).astype(jnp.int32)


def raised(values, key, source, target, shards_of, factor):
    def block_of(dim):
        return (jnp.arange(values.shape[dim]) // (values.shape[dim] // shards_of)).reshape((-1,) + (1,) * (values.ndim - 1 - dim))

    near = jax.random.permutation(key, shards_of)[block_of(target)]
    second = (block_of(target) + shards_of // 2) % shards_of
    return jnp.where((block_of(source) == near) | (block_of(source) == second), factor * values, values)


def level_of(rng, extent, cuts, smallest, high):
    def one(dim, blocks):
        draws = jax.random.uniform(jax.random.fold_in(jax.random.fold_in(rng, 6), dim), (blocks,), jnp.float32, smallest / len(cuts), high / len(cuts))
        return jnp.repeat(jnp.exp(draws), extent[dim] // blocks).reshape((-1,) + (1,) * (len(extent) - dim - 1))

    gain = one(*cuts[0])
    for cut in cuts[1:]:
        gain = gain * one(*cut)
    return gain


def noise(own_key, dims, scale, most, pieces=(), kind=jnp.bfloat16):
    values = jax.random.normal(own_key, dims, jnp.float32) * scale
    if len(pieces) > 0:
        values = level_of(own_key, dims, pieces, -0.22, 0.18) * values
    return jnp.clip(values, min=-most, max=most).astype(kind)


def heavy_noise(stream_key, extent, spread, bound, shards, heavy, held_as=jnp.bfloat16):
    result = spread * jax.random.normal(stream_key, extent, jnp.float32)
    if shards:
        result = result * level_of(stream_key, extent, shards, -0.22, 0.18)
    return jnp.clip(raised(result, jax.random.fold_in(stream_key, 3), *heavy), -bound, bound).astype(held_as)


def setup_inputs(seed: int = 0) -> dict:
    splits = jax.random.split(jax.random.key(seed), 13)
    return {
        "inputs": noise(splits[0], (TOKENS, D), 1.0, 6.0, ((0, 32),), jnp.float32),
        "lengths": draw_lengths(jax.random.fold_in(splits[12], 71), 0),
        "qkv_weight": noise(splits[2], (LAYERS, 3, D, D), D ** -0.5, 0.21875, ((2, 8), (3, 4))),
        "qv_bias": noise(splits[3], (LAYERS, 2, D), 0.5, 3.0, ((2, 4),), jnp.float32),
        "proj_weight": noise(splits[4], (LAYERS, D, D), (D // 64) ** -0.5, 1.75, ((1, 4), (2, 8))),
        "branch_bias": noise(splits[5], (LAYERS, 2, D), 0.5, 3.0, (), jnp.float32),
        "up_weight": noise(splits[6], (LAYERS, D, FF), D ** -0.5, 0.21875, ((1, 8), (2, 4))),
        "up_bias": noise(splits[7], (LAYERS, FF), 0.5, 3.0, ((1, 4),), jnp.float32),
        "down_weight": noise(splits[8], (LAYERS, FF, D), FF ** -0.5, 0.109375, ((1, 4), (2, 8))),
        "norm_gain": jnp.clip(1.0 + 0.1 * jax.random.normal(splits[9], (LAYERS, 2, D), jnp.float32), 0.5, 1.5),
        "norm_bias": noise(splits[10], (LAYERS, 2, D), 0.5, 3.0, (), jnp.float32),
        "cotangent": heavy_noise(splits[11], (TOKENS, D), 1.0, 6.0, ((0, 32),), (0, 1, 32, 2.75), jnp.float32),
    }


norm_eps = 1e-12
half_root = 0.7071067811865476
inv_root = 0.3989422804014327

def layer_norm(residual):
    centred = residual - lax.optimization_barrier(jnp.mean(residual, axis=-1, keepdims=True))
    inverse = lax.rsqrt(lax.optimization_barrier(jnp.mean(centred * centred, axis=-1, keepdims=True)) + norm_eps)
    return (centred * inverse, inverse)

def norm_back(upstream, normed, inverse, gain_row):
    scaled = upstream * gain_row
    return inverse * (scaled - lax.optimization_barrier(jnp.mean(scaled, axis=-1, keepdims=True)) - normed * lax.optimization_barrier(jnp.mean(scaled * normed, axis=-1, keepdims=True)))

def gelu_value(pre_act):
    return 0.5 * pre_act * (1.0 + lax.erf(pre_act * half_root))

def gelu_slope(pre_act):
    return 0.5 * (1.0 + lax.erf(pre_act * half_root)) + pre_act * jnp.exp(-0.5 * pre_act * pre_act) * inv_root

def reference(inputs, lengths, qkv_weight, qv_bias, proj_weight, branch_bias, up_weight, up_bias, down_weight, norm_gain, norm_bias, cotangent):
    score_scale = 1.0 / math.sqrt(HD)
    seq_total = lengths.shape[0]
    width = inputs.shape[1]
    positions = jnp.arange(L, dtype=jnp.int32)

    def score_block(queries, key_rows, key_valid):
        raw_scores = jnp.einsum('qhc,khc->hqk', queries.astype(jnp.float32), key_rows.astype(jnp.float32)) * score_scale
        return jnp.where(key_valid[None, None, :], raw_scores, -1e+30)

    def one_sequence(totals, item):
        seq_rows, seq_grad, seq_length = item
        key_valid = positions < seq_length
        stored = []
        hidden = seq_rows
        for layer_index in range(LAYERS):
            rounded = hidden.astype(jnp.bfloat16)
            mixed_rows = jnp.einsum('rd,jde->jre', rounded.astype(jnp.float32), qkv_weight[layer_index].astype(jnp.float32))
            queries = (mixed_rows[0] + qv_bias[layer_index, 0]).astype(jnp.bfloat16).reshape(L, HEADS, HD)
            key_rows = mixed_rows[1].astype(jnp.bfloat16).reshape(L, HEADS, HD)
            values = (mixed_rows[2] + qv_bias[layer_index, 1]).astype(jnp.bfloat16).reshape(L, HEADS, HD)
            scores = score_block(queries, key_rows, key_valid)
            row_peak = lax.optimization_barrier(jnp.max(scores, axis=-1, keepdims=True))
            log_total = row_peak + jnp.log(lax.optimization_barrier(jnp.sum(jnp.exp(scores - row_peak), axis=-1, keepdims=True)))
            soft_weights = jnp.exp(scores - log_total).astype(jnp.bfloat16)
            context = jnp.einsum('hqk,khc->qhc', soft_weights.astype(jnp.float32), values.astype(jnp.float32)).astype(jnp.bfloat16).reshape(L, width)
            residual = hidden + jnp.dot(context, proj_weight[layer_index], preferred_element_type=jnp.float32) + branch_bias[layer_index, 0]
            normed_one, inverse_one = layer_norm(residual)
            middle = normed_one * norm_gain[layer_index, 0] + norm_bias[layer_index, 0]
            middle_rows = middle.astype(jnp.bfloat16)
            pre_act = jnp.dot(middle_rows, up_weight[layer_index], preferred_element_type=jnp.float32) + up_bias[layer_index]
            active = gelu_value(pre_act).astype(jnp.bfloat16)
            residual_two = middle + jnp.dot(active, down_weight[layer_index], preferred_element_type=jnp.float32) + branch_bias[layer_index, 1]
            normed_two, inverse_two = layer_norm(residual_two)
            stored.append((rounded, queries, key_rows, values, log_total, context, normed_one, inverse_one, middle_rows, pre_act, active, normed_two, inverse_two))
            hidden = normed_two * norm_gain[layer_index, 1] + norm_bias[layer_index, 1]
        upstream = seq_grad
        totals = list(totals)
        for layer_index in reversed(range(LAYERS)):
            rounded, queries, key_rows, values, log_total, context, normed_one, inverse_one, middle_rows, pre_act, active, normed_two, inverse_two = stored[layer_index]
            totals[7] = totals[7].at[layer_index, 1].add(lax.optimization_barrier(jnp.sum(upstream * normed_two, axis=0)))
            totals[8] = totals[8].at[layer_index, 1].add(lax.optimization_barrier(jnp.sum(upstream, axis=0)))
            dres_two = norm_back(upstream, normed_two, inverse_two, norm_gain[layer_index, 1])
            totals[3] = totals[3].at[layer_index, 1].add(lax.optimization_barrier(jnp.sum(dres_two, axis=0)))
            dres_two_b = dres_two.astype(jnp.bfloat16)
            totals[6] = totals[6].at[layer_index].add(jnp.dot(active.T, dres_two_b, preferred_element_type=jnp.float32))
            dpre = jnp.dot(dres_two_b, down_weight[layer_index].T, preferred_element_type=jnp.float32) * gelu_slope(pre_act)
            totals[5] = totals[5].at[layer_index].add(lax.optimization_barrier(jnp.sum(dpre, axis=0)))
            dpre_b = dpre.astype(jnp.bfloat16)
            totals[4] = totals[4].at[layer_index].add(jnp.dot(middle_rows.T, dpre_b, preferred_element_type=jnp.float32))
            dmiddle = dres_two + jnp.dot(dpre_b, up_weight[layer_index].T, preferred_element_type=jnp.float32)
            totals[7] = totals[7].at[layer_index, 0].add(lax.optimization_barrier(jnp.sum(dmiddle * normed_one, axis=0)))
            totals[8] = totals[8].at[layer_index, 0].add(lax.optimization_barrier(jnp.sum(dmiddle, axis=0)))
            dres_one = norm_back(dmiddle, normed_one, inverse_one, norm_gain[layer_index, 0])
            totals[3] = totals[3].at[layer_index, 0].add(lax.optimization_barrier(jnp.sum(dres_one, axis=0)))
            dres_one_b = dres_one.astype(jnp.bfloat16)
            totals[2] = totals[2].at[layer_index].add(jnp.dot(context.T, dres_one_b, preferred_element_type=jnp.float32))
            dcontext = jnp.dot(dres_one_b, proj_weight[layer_index].T, preferred_element_type=jnp.float32).astype(jnp.bfloat16).reshape(L, HEADS, HD)
            scores = score_block(queries, key_rows, key_valid)
            probs_full = jnp.exp(scores - log_total)
            dprob = jnp.einsum('qhc,khc->hqk', dcontext.astype(jnp.float32), values.astype(jnp.float32))
            dscore = (probs_full * (dprob - lax.optimization_barrier(jnp.sum(probs_full * dprob, axis=-1, keepdims=True))) * score_scale).astype(jnp.bfloat16)
            dquery = jnp.einsum('hqk,khc->qhc', dscore.astype(jnp.float32), key_rows.astype(jnp.float32))
            dkey = jnp.einsum('hqk,qhc->khc', dscore.astype(jnp.float32), queries.astype(jnp.float32))
            dvalue = jnp.einsum('hqk,qhc->khc', probs_full.astype(jnp.bfloat16).astype(jnp.float32), dcontext.astype(jnp.float32))
            dmixed_full = jnp.stack([dquery, dkey, dvalue]).reshape(3, L, width)
            totals[1] = totals[1].at[layer_index].add(jnp.stack([lax.optimization_barrier(jnp.sum(dmixed_full[0], axis=0)), lax.optimization_barrier(jnp.sum(dmixed_full[2], axis=0))]))
            dmixed = dmixed_full.astype(jnp.bfloat16)
            totals[0] = totals[0].at[layer_index].add(jnp.einsum('rd,jre->jde', rounded.astype(jnp.float32), dmixed.astype(jnp.float32)))
            upstream = dres_one + jnp.einsum('jre,jde->rd', dmixed.astype(jnp.float32), qkv_weight[layer_index].astype(jnp.float32))
        return (tuple(totals), (hidden, upstream))
    zero_totals = (jnp.zeros(qkv_weight.shape, jnp.float32), jnp.zeros(qv_bias.shape, jnp.float32), jnp.zeros(proj_weight.shape, jnp.float32), jnp.zeros(branch_bias.shape, jnp.float32), jnp.zeros(up_weight.shape, jnp.float32), jnp.zeros(up_bias.shape, jnp.float32), jnp.zeros(down_weight.shape, jnp.float32), jnp.zeros(norm_gain.shape, jnp.float32), jnp.zeros(norm_bias.shape, jnp.float32))
    totals, (out_rows, grad_rows) = lax.scan(one_sequence, zero_totals, (inputs.reshape(seq_total, L, width), cotangent.reshape(seq_total, L, width), lengths))
    return (out_rows.reshape(seq_total * L, width), grad_rows.reshape(seq_total * L, width), totals[0], totals[1], totals[2], totals[3], totals[4], totals[5], totals[6], totals[7], totals[8])
```

```python
import functools
import math
from types import SimpleNamespace

import jax
import jax.numpy as jnp
from jax import lax
from jax.experimental import pallas as pl
from jax.experimental.pallas import tpu as pltpu
from jax.sharding import PartitionSpec as P

MESH = pl.DeviceIdType.MESH
BF = jnp.bfloat16
F32 = jnp.float32
HD = 64
CH = 2

norm_eps = 1e-12
half_root = 0.7071067811865476
inv_root = 0.3989422804014327


def layer_norm(residual):
    centred = residual - jnp.mean(residual, axis=-1, keepdims=True)
    inverse = lax.rsqrt(jnp.mean(centred * centred, axis=-1, keepdims=True) + norm_eps)
    return (centred * inverse, inverse)


def norm_back(upstream, normed, inverse, gain_row):
    scaled = upstream * gain_row
    return inverse * (
        scaled
        - jnp.mean(scaled, axis=-1, keepdims=True)
        - normed * jnp.mean(scaled * normed, axis=-1, keepdims=True)
    )


def gelu_value(pre_act):
    return 0.5 * pre_act * (1.0 + lax.erf(pre_act * half_root))


def gelu_slope(pre_act):
    return (
        0.5 * (1.0 + lax.erf(pre_act * half_root))
        + pre_act * jnp.exp(-0.5 * pre_act * pre_act) * inv_root
    )


def nn_dot(left, right):
    return jnp.dot(left, right, preferred_element_type=F32)


def nt_dot(left, right):
    return lax.dot_general(left, right, (((1,), (1,)), ((), ())), preferred_element_type=F32)


def tn_dot(left, right):
    return lax.dot_general(left, right, (((0,), (0,)), ((), ())), preferred_element_type=F32)


def turned(block):
    size = block.shape[1]
    row = lax.broadcasted_iota(jnp.int32, (size, size), 0)
    col = lax.broadcasted_iota(jnp.int32, (size, size), 1)
    return nt_dot(jnp.where(row == col, 1.0, 0.0).astype(BF), block).astype(BF)


def send(src, dst, send_sem, recv_sem, axis, target):
    return pltpu.make_async_remote_copy(
        src_ref=src,
        dst_ref=dst,
        send_sem=send_sem,
        recv_sem=recv_sem,
        device_id={axis: target},
        device_id_type=MESH,
    )


def ways(me, n):
    return ((0, me, me + 1), (1, n - 1 - me, me - 1))


class ChainGather:
    def __init__(self, buf, me, n, ssem, rsem):
        self.buf, self.me, self.n, self.ssem, self.rsem = buf, me, n, ssem, rsem
        self.chunk = buf.shape[1] // CH

    def link(self, way, s, c, pos, target):
        block = pos - s
        block = block if way == 0 else self.n - 1 - block
        view = self.buf.at[block, pl.ds(c * self.chunk, self.chunk)]
        sems = self.ssem.at[way, s, c], self.rsem.at[way, s, c]
        return send(view, view, *sems, "tensor", target)

    def step(self, s, c):
        for way, pos, target in ways(self.me, self.n):

            @pl.when(jnp.logical_and(pos >= s, pos < self.n - 1))
            def _(way=way, pos=pos, target=target):
                if s > 0:
                    self.link(way, s - 1, c, pos - 1, target).wait_recv()
                self.link(way, s, c, pos, target).start()

    def steps(self, s):
        for c in range(CH):
            self.step(s, c)

    def last(self):
        for way, pos, target in ways(self.me, self.n):

            @pl.when(pos == self.n - 1)
            def _(way=way, pos=pos, target=target):
                for s in range(self.n - 1):
                    for c in range(CH):
                        self.link(way, s, c, pos - 1, target).wait_recv()

    def finish(self):
        for s in range(self.n - 1):
            for way, pos, target in ways(self.me, self.n):

                @pl.when(jnp.logical_and(pos >= s, pos < self.n - 1))
                def _(way=way, pos=pos, target=target):
                    for c in range(CH):
                        self.link(way, s, c, pos, target).wait_send()


class ChainReduce:
    def __init__(self, terms, me, n, sbuf, rbuf, ssem, rsem):
        self.terms, self.me, self.n = terms, me, n
        self.sbuf, self.rbuf, self.ssem, self.rsem = sbuf, rbuf, ssem, rsem
        self.chunk = terms.shape[1] // CH

    def part(self, c):
        return pl.ds(c * self.chunk, self.chunk)

    def link(self, way, s, c, target):
        return send(
            self.sbuf.at[way, s, self.part(c)],
            self.rbuf.at[way, s, self.part(c)],
            self.ssem.at[way, s, c],
            self.rsem.at[way, s, c],
            "tensor",
            target,
        )

    def step(self, s, c):
        for way, pos, target in ways(self.me, self.n):
            owner = self.n - 1 - s + pos
            block = owner if way == 0 else self.n - 1 - owner

            @pl.when(pos <= s)
            def _(way=way, pos=pos, target=target, block=block):
                if s == 0:
                    self.sbuf[way, s, self.part(c)] = self.terms[block, self.part(c)].astype(BF)
                else:

                    @pl.when(pos == 0)
                    def _():
                        self.sbuf[way, s, self.part(c)] = self.terms[block, self.part(c)].astype(BF)

                    @pl.when(pos > 0)
                    def _():
                        self.link(way, s - 1, c, target).wait_recv()
                        got = self.rbuf[way, s - 1, self.part(c)].astype(F32)
                        self.sbuf[way, s, self.part(c)] = (
                            self.terms[block, self.part(c)] + got
                        ).astype(BF)

                self.link(way, s, c, target).start()

    def steps(self, s):
        for c in range(CH):
            self.step(s, c)

    def total(self, c, acc):
        acc[self.part(c)] = self.terms[self.me, self.part(c)]
        for way, pos, target in ways(self.me, self.n):

            @pl.when(pos > 0)
            def _(way=way, target=target):
                self.link(way, self.n - 2, c, target).wait_recv()
                acc[self.part(c)] += self.rbuf[way, self.n - 2, self.part(c)].astype(F32)

    def finish(self):
        for s in range(self.n - 1):
            for way, pos, target in ways(self.me, self.n):

                @pl.when(pos <= s)
                def _(way=way, target=target):
                    for c in range(CH):
                        self.link(way, s, c, target).wait_send()


class PlaneGather:
    def __init__(self, buf, mine, dp, ssem, rsem):
        self.buf, self.mine, self.dp, self.ssem, self.rsem = buf, mine, dp, ssem, rsem
        self.chips = dp // 2
        self.partner = mine + 1 - 2 * lax.rem(mine, 2)

    def chip(self, k):
        view = self.buf.at[self.mine]
        target = lax.rem(self.mine + 2 * k, self.dp)
        return send(view, view, self.ssem.at[k], self.rsem.at[k], "dp", target)

    def core(self, k):
        view = self.buf.at[lax.rem(self.mine + self.dp - 2 * k, self.dp)]
        sems = self.ssem.at[self.chips + k], self.rsem.at[self.chips + k]
        return send(view, view, *sems, "dp", self.partner)

    def start(self):
        for k in range(1, self.chips):
            self.chip(k).start()
        self.core(0).start()

    def relay(self):
        for k in range(1, self.chips):
            self.chip(k).wait_recv()
            self.core(k).start()

    def last(self):
        for k in range(self.chips):
            self.core(k).wait_recv()

    def finish(self):
        for k in range(self.chips):
            if k > 0:
                self.chip(k).wait_send()
            self.core(k).wait_send()


class PlaneReduce:
    def __init__(self, parts, got, summed, land, mine, dp, csem, drsem, xsem, xrsem):
        self.parts, self.got, self.summed, self.land = parts, got, summed, land
        self.mine, self.dp, self.chips = mine, dp, dp // 2
        self.partner = mine + 1 - 2 * lax.rem(mine, 2)
        self.sems = csem, drsem, xsem, xrsem

    def core(self, k):
        part = self.parts.at[lax.rem(self.partner + 2 * k, self.dp)]
        return send(part, self.got.at[k], self.sems[0].at[k], self.sems[1].at[k], "dp", self.partner)

    def chip(self, k):
        target = lax.rem(self.mine + 2 * k, self.dp)
        sems = self.sems[2].at[k], self.sems[3].at[k]
        return send(self.summed.at[k], self.land.at[k], *sems, "dp", target)

    def start(self):
        for k in list(range(1, self.chips)) + [0]:
            self.core(k).start()

    def pair(self, k):
        self.core(k).wait_recv()
        own = self.parts[lax.rem(self.mine + 2 * k, self.dp)].astype(F32)
        return own + self.got[k].astype(F32)

    def spread(self):
        for k in range(1, self.chips):
            self.summed[k] = self.pair(k).astype(BF)
            self.chip(k).start()

    def total(self):
        total = self.pair(0)
        for k in range(1, self.chips):
            self.chip(k).wait_recv()
            total = total + self.land[k].astype(F32)
        return total

    def finish(self):
        for k in range(self.chips):
            self.core(k).wait_send()
            if k > 0:
                self.chip(k).wait_send()


def joined(value):
    parts, rows, columns = value.shape
    if rows % 16 == 0:
        return value.reshape(parts * rows, columns)
    return jnp.concatenate([value[d] for d in range(parts)], axis=0)


def put_parts(ref, value, *where):
    parts, rows = ref.shape[0], ref.shape[-2]
    for d in range(parts):
        ref[(d,) + where] = value[d * rows : (d + 1) * rows].astype(BF)


def layer_kernel(n, dp, names, *refs):
    r = SimpleNamespace(**dict(zip(names, refs)))
    me = lax.axis_index("tensor")
    mine = lax.axis_index("dp")
    chips = dp // 2
    chip = lax.div(mine, 2)
    core_mate = mine + 1 - 2 * lax.rem(mine, 2)
    pair_mate = me + 1 - 2 * lax.rem(me, 2)
    far = lax.rem(me + n // 2, n)
    own_rows, width = r.x.shape
    local = r.q.shape[1]
    units = r.ub.shape[-1]
    chunk = own_rows // CH
    scale = 1.0 / math.sqrt(HD)

    loads = {
        name: pltpu.make_async_copy(src, dst, r.lsem.at[k])
        for k, (name, src, dst) in enumerate(
            [
                ("x", r.x_h, r.x),
                ("qkv", r.qkv_h, r.qkv.at[mine]),
                ("proj", r.proj_h, r.pv),
                ("down", r.down_h, r.dv),
                ("up", r.up_h, r.ud.at[0, mine, 0]),
                ("ub", r.ub_h, r.ub.at[0]),
                ("qvb", r.qvb_h, r.qvb),
                ("bb", r.bb_h, r.bb),
                ("gain", r.gain_h, r.gain),
                ("nb", r.nb_h, r.nb),
                ("cot", r.cot_h, r.cot),
            ]
        )
    }
    for copy in loads.values():
        copy.start()

    barrier = pltpu.get_barrier_semaphore()
    for k in range(1, n):
        pl.semaphore_signal(
            barrier, inc=1, device_id={"tensor": lax.rem(me + k, n)}, device_id_type=MESH
        )
    for k in range(1, chips):
        pl.semaphore_signal(
            barrier, inc=1, device_id={"dp": lax.rem(mine + 2 * k, dp)}, device_id_type=MESH
        )
    pl.semaphore_signal(barrier, inc=1, device_id={"dp": core_mate}, device_id_type=MESH)

    loads["x"].wait()
    r.xr[me] = r.x[...].astype(BF)
    loads["proj"].wait()
    r.pj[mine] = turned(r.pv[...])
    loads["down"].wait()
    r.ud[0, mine, 1] = turned(r.dv[...])
    for name in ("qkv", "up", "ub"):
        loads[name].wait()
    pl.semaphore_wait(barrier, n - 1 + chips)

    xg = ChainGather(r.xr, me, n, r.xg_s, r.xg_r)
    gathers = [
        PlaneGather(buf, mine, dp, r.w_s.at[k], r.w_r.at[k])
        for k, buf in enumerate((r.qkv, r.pj, r.ud.at[0], r.ud.at[1]))
    ]
    g_qkv, g_proj, g_ud, g_far = gathers

    def far_copy(k):
        src, dst = (
            (r.ud.at[0, mine, 0], r.ud.at[1, mine, 0]),
            (r.ud.at[0, mine, 1], r.ud.at[1, mine, 1]),
            (r.ub.at[0], r.ub.at[1]),
            (r.zs, r.zr),
        )[k]
        return send(src, dst, r.z_s.at[k], r.z_r.at[k], "tensor", far)

    def pair_copy(phase, c, src, dst):
        return send(
            src.at[pl.ds(c * chunk, chunk)],
            dst.at[pl.ds(c * chunk, chunk)],
            r.p_s.at[phase, c],
            r.p_r.at[phase, c],
            "tensor",
            pair_mate,
        )

    def rows_of(c):
        return pl.ds(c * chunk, chunk)

    xg.steps(0)
    g_qkv.start()
    g_proj.start()
    far_copy(0).start()
    xg.steps(1)
    g_qkv.relay()
    g_proj.relay()
    xg.steps(2)
    far_copy(1).start()
    far_copy(2).start()
    g_ud.start()
    for name in ("qvb", "bb", "gain", "nb", "cot"):
        loads[name].wait()
    g_qkv.last()
    xg.last()

    rounded = joined(r.xr[...])
    r.q[...] = (nn_dot(rounded, joined(r.qkv[:, 0])) + r.qvb[0:1, :]).astype(BF)
    r.k[...] = nn_dot(rounded, joined(r.qkv[:, 1])).astype(BF)
    r.v[...] = (nn_dot(rounded, joined(r.qkv[:, 2])) + r.qvb[1:2, :]).astype(BF)
    seq_rows = r.q.shape[0]
    valid = lax.broadcasted_iota(jnp.int32, (seq_rows, seq_rows), 1) < r.lengths[0]
    heads = local // HD
    for head in range(heads):
        cols = slice(head * HD, (head + 1) * HD)
        scores = jnp.where(valid, nt_dot(r.q[:, cols], r.k[:, cols]) * scale, -1e30)
        weights = jnp.exp(scores - jnp.max(scores, axis=-1, keepdims=True))
        prob = weights * (1.0 / jnp.sum(weights, axis=-1, keepdims=True))
        r.prob[head] = prob
        r.ctx[:, cols] = nn_dot(prob.astype(BF), r.v[:, cols]).astype(BF)
    g_proj.last()
    r.terms[...] = nt_dot(r.ctx[...], joined(r.pj[...])).reshape(r.terms.shape)

    red = ChainReduce(r.terms, me, n, r.s1, r.r1, r.r1_s, r.r1_r)
    red.steps(0)
    far_copy(0).wait_recv()
    far_copy(1).wait_recv()
    g_far.start()
    red.steps(1)
    g_ud.relay()
    red.steps(2)

    for c in range(CH):
        part = rows_of(c)
        red.total(c, r.acc)
        normed, inverse = layer_norm(r.x[part] + r.acc[part] + r.bb[0:1, :])
        middle = normed * r.gain[0:1, :] + r.nb[0:1, :]
        r.n1[part] = normed
        r.i1[part] = inverse
        r.mid[part] = middle
        r.m_all[0, part] = middle.astype(BF)
        pair_copy(0, c, r.m_all.at[0], r.m_all.at[1]).start()
    g_far.relay()
    g_ud.last()
    far_copy(2).wait_recv()

    def up_rows(group, h):
        cols = slice(h * units, (h + 1) * units)
        pre = nn_dot(r.m_all[group], joined(r.ud[h, :, 0])) + r.ub[h]
        r.pre[group, :, cols] = pre
        r.act[group, :, cols] = gelu_value(pre).astype(BF)

    def down_rows(group):
        return nt_dot(r.act[group, :, :units], joined(r.ud[0, :, 1])) + nt_dot(
            r.act[group, :, units:], joined(r.ud[1, :, 1])
        )

    up_rows(0, 0)
    g_far.last()
    up_rows(0, 1)
    for c in range(CH):
        pair_copy(0, c, r.m_all.at[0], r.m_all.at[1]).wait_recv()
    up_rows(1, 0)
    up_rows(1, 1)
    r.ps[0] = down_rows(1).astype(BF)
    for c in range(CH):
        pair_copy(1, c, r.ps.at[0], r.pr.at[0]).start()
    r.acc[...] = down_rows(0)
    for group in range(2):
        for h in range(2):
            cols = slice(h * units, (h + 1) * units)
            r.pre[group, :, cols] = gelu_slope(r.pre[group, :, cols])

    for c in range(CH):
        part = rows_of(c)
        pair_copy(1, c, r.ps.at[0], r.pr.at[0]).wait_recv()
        normed, inverse = layer_norm(
            r.mid[part] + r.acc[part] + r.pr[0, part].astype(F32) + r.bb[1:2, :]
        )
        dres = norm_back(r.cot[part], normed, inverse, r.gain[1:2, :])
        r.d_all[0, part] = dres.astype(BF)
        pair_copy(2, c, r.d_all.at[0], r.d_all.at[1]).start()
        r.dres[part] = dres
        r.acc[part] = normed
    r.hidden_o[...] = r.acc[...] * r.gain[1:2, :] + r.nb[1:2, :]
    r.sums[3:4, :] = jnp.sum(r.cot[...] * r.acc[...], axis=0, keepdims=True)
    r.sums[4:5, :] = jnp.sum(r.cot[...], axis=0, keepdims=True)
    r.sums[5:6, :] = jnp.sum(r.dres[...], axis=0, keepdims=True)

    def back_rows(group, h):
        cols = slice(h * units, (h + 1) * units)
        dpre = nn_dot(r.d_all[group], joined(r.ud[h, :, 1])) * r.pre[group, :, cols]
        r.dpre[group, :, cols] = dpre.astype(BF)
        total = jnp.sum(dpre, axis=0, keepdims=True)
        r.sums[6 + h : 7 + h, :] = total if group == 0 else r.sums[6 + h : 7 + h, :] + total

    def up_back(group):
        return nt_dot(r.dpre[group, :, :units], joined(r.ud[0, :, 0])) + nt_dot(
            r.dpre[group, :, units:], joined(r.ud[1, :, 0])
        )

    back_rows(0, 0)
    back_rows(0, 1)
    for c in range(CH):
        pair_copy(2, c, r.d_all.at[0], r.d_all.at[1]).wait_recv()
    back_rows(1, 0)
    back_rows(1, 1)
    r.ps[1] = up_back(1).astype(BF)
    for c in range(CH):
        pair_copy(3, c, r.ps.at[1], r.pr.at[1]).start()
    r.acc[...] = up_back(0) + r.dres[...]

    reduces = [
        PlaneReduce(
            r.g.at[h], r.gp.at[h], r.gs.at[h], r.gl.at[h], mine, dp,
            r.gc_s.at[h], r.gc_r.at[h], r.gx_s.at[h], r.gx_r.at[h],
        )
        for h in range(2)
    ]
    for h in (1, 0):
        cols = slice(h * units, (h + 1) * units)
        put_parts(r.g.at[h], tn_dot(joined(r.d_all[...]), joined(r.act[:, :, cols])), 1)
        put_parts(r.g.at[h], tn_dot(joined(r.m_all[...]), joined(r.dpre[:, :, cols])), 0)
        reduces[h].start()

    dg = ChainGather(r.dr, me, n, r.dg_s, r.dg_r)
    for c in range(CH):
        part = rows_of(c)
        pair_copy(3, c, r.ps.at[1], r.pr.at[1]).wait_recv()
        dmid = r.acc[part] + r.pr[1, part].astype(F32)
        dres = norm_back(dmid, r.n1[part], r.i1[part], r.gain[0:1, :])
        r.dr[me, part] = dres.astype(BF)
        dg.step(0, c)
        r.acc[part] = dmid
        r.dres[part] = dres
    reduces[1].spread()
    dg.steps(1)
    reduces[0].spread()
    r.sums[0:1, :] = jnp.sum(r.acc[...] * r.n1[...], axis=0, keepdims=True)
    r.sums[1:2, :] = jnp.sum(r.acc[...], axis=0, keepdims=True)
    r.sums[2:3, :] = jnp.sum(r.dres[...], axis=0, keepdims=True)

    def sum_mate():
        return send(r.sums, r.sp, r.m_s.at[0], r.m_r.at[0], "dp", core_mate)

    def sum_chip(k):
        view = r.sc.at[chip]
        sems = r.sc_s.at[k], r.sc_r.at[k]
        return send(view, view, *sems, "dp", lax.rem(mine + 2 * k, dp))

    def sum_z(k):
        view = r.st.at[me]
        return send(view, view, r.st_s.at[k], r.st_r.at[k], "tensor", lax.rem(me + k, n))

    def bias_mate():
        return send(r.b, r.bp, r.m_s.at[1], r.m_r.at[1], "dp", core_mate)

    def bias_chip(k):
        view = r.bc.at[chip]
        sems = r.bc_s.at[k], r.bc_r.at[k]
        return send(view, view, *sems, "dp", lax.rem(mine + 2 * k, dp))

    sum_mate().start()
    dg.steps(2)
    sum_mate().wait_recv()
    r.sc[chip] = r.sums[...] + r.sp[...]
    for k in range(1, chips):
        sum_chip(k).start()
    dg.last()

    dres_all = joined(r.dr[...])
    r.dctx[...] = nn_dot(dres_all, joined(r.pj[...])).astype(BF)
    r.b[...] = jnp.zeros_like(r.b)
    for head in range(heads):
        cols = slice(head * HD, (head + 1) * HD)
        prob = r.prob[head]
        dc = r.dctx[:, cols]
        dprob = nt_dot(dc, r.v[:, cols])
        inner = jnp.sum(prob * dprob, axis=-1, keepdims=True)
        dscore = (prob * (dprob - inner) * scale).astype(BF)
        dquery = nn_dot(dscore, r.k[:, cols])
        dvalue = tn_dot(prob.astype(BF), dc)
        r.dm[0, :, cols] = dquery.astype(BF)
        r.dm[1, :, cols] = tn_dot(dscore, r.q[:, cols]).astype(BF)
        r.dm[2, :, cols] = dvalue.astype(BF)
        r.b[0:1, cols] = jnp.sum(dquery, axis=0, keepdims=True)
        r.b[1:2, cols] = jnp.sum(dvalue, axis=0, keepdims=True)
    dx = nt_dot(r.dm[0], joined(r.qkv[:, 0]))
    for j in range(1, 3):
        dx = dx + nt_dot(r.dm[j], joined(r.qkv[:, j]))
    r.terms[...] = dx.reshape(r.terms.shape)

    red_x = ChainReduce(r.terms, me, n, r.s2, r.r2, r.r2_s, r.r2_r)
    red_x.steps(0)
    attn = PlaneReduce(
        r.a, r.ap, r.as_, r.al, mine, dp, r.ac_s, r.ac_r, r.ax_s, r.ax_r
    )
    rounded = joined(r.xr[...])
    for j in range(3):
        put_parts(r.a, tn_dot(rounded, r.dm[j]), j)
    put_parts(r.a, tn_dot(joined(r.dr[...]), r.ctx[...]), 3)
    attn.start()
    bias_mate().start()
    red_x.steps(1)
    attn.spread()
    bias_mate().wait_recv()
    r.bc[chip] = r.b[...] + r.bp[...]
    for k in range(1, chips):
        bias_chip(k).start()
    r.zs[...] = reduces[1].total().astype(BF)
    far_copy(3).start()
    red_x.steps(2)

    for k in range(1, chips):
        sum_chip(k).wait_recv()
    total = r.sc[0]
    for k in range(1, chips):
        total = total + r.sc[k]
    r.st[me] = total
    for k in range(1, n):
        sum_z(k).start()
    near_total = reduces[0].total()
    r.ud_o[...] = near_total

    for c in range(CH):
        red_x.total(c, r.acc)
    r.dx_o[...] = r.acc[...] + r.dres[...]
    for k in range(1, n):
        sum_z(k).wait_recv()
    total = r.st[0]
    for k in range(1, n):
        total = total + r.st[k]
    r.sums_o[0:6, :] = total[0:6]
    r.sums_o[6:7, :] = r.st[me, 6:7] + r.st[far, 7:8]
    r.sums_o[7:8, :] = jnp.zeros_like(r.sums_o[7:8, :])
    for k in range(1, chips):
        bias_chip(k).wait_recv()
    total = r.bc[0]
    for k in range(1, chips):
        total = total + r.bc[k]
    r.bias_o[...] = total
    r.attn_o[...] = attn.total()
    far_copy(3).wait_recv()
    r.ud_o[...] += r.zr[...].astype(F32)

    xg.finish()
    dg.finish()
    red.finish()
    red_x.finish()
    for gather in gathers:
        gather.finish()
    for reduce in reduces + [attn]:
        reduce.finish()
    for k in range(4):
        far_copy(k).wait_send()
    for c in range(CH):
        pair_copy(0, c, r.m_all.at[0], r.m_all.at[1]).wait_send()
        pair_copy(1, c, r.ps.at[0], r.pr.at[0]).wait_send()
        pair_copy(2, c, r.d_all.at[0], r.d_all.at[1]).wait_send()
        pair_copy(3, c, r.ps.at[1], r.pr.at[1]).wait_send()
    sum_mate().wait_send()
    bias_mate().wait_send()
    for k in range(1, chips):
        sum_chip(k).wait_send()
        bias_chip(k).wait_send()
    for k in range(1, n):
        sum_z(k).wait_send()


def store_kernel(
    hidden, dx, attn, ud, sums, bias,
    hidden_o, dx_o, qkv_o, qvb_o, proj_o, branch_o, up_o, ub_o, down_o, gain_o, nb_o,
):
    hidden_o[...] = hidden[...]
    dx_o[...] = dx[...]
    qkv_o[...] = attn[0:3]
    proj_o[...] = attn[3].T
    up_o[...] = ud[0]
    down_o[...] = ud[1].T
    qvb_o[...] = bias[0:2, :]
    ub_o[...] = sums[6:7, :]
    for j in range(2):
        gain_o[j : j + 1, :] = sums[3 * j : 3 * j + 1, :]
        nb_o[j : j + 1, :] = sums[3 * j + 1 : 3 * j + 2, :]
        branch_o[j : j + 1, :] = sums[3 * j + 2 : 3 * j + 3, :]


def per_device(
    inputs,
    lengths,
    qkv_weight,
    qv_bias,
    proj_weight,
    branch_bias,
    up_weight,
    up_bias,
    down_weight,
    norm_gain,
    norm_bias,
    cotangent,
):
    n = lax.axis_size("tensor")
    dp = lax.axis_size("dp")
    rows, width = inputs.shape
    shard, local = qkv_weight.shape[2:]
    units = up_weight.shape[2]
    chips = dp // 2
    seq = rows * n
    heads = local // HD
    dma = pltpu.SemaphoreType.DMA

    operands = {
        "lengths": lengths,
        "x_h": inputs,
        "qkv_h": qkv_weight[0],
        "qvb_h": qv_bias[0],
        "proj_h": proj_weight[0],
        "bb_h": branch_bias[0],
        "up_h": up_weight[0],
        "ub_h": up_bias,
        "down_h": down_weight[0],
        "gain_h": norm_gain[0],
        "nb_h": norm_bias[0],
        "cot_h": cotangent,
    }
    outs = {
        "hidden_o": (rows, width),
        "dx_o": (rows, width),
        "attn_o": (4, shard, local),
        "ud_o": (2, shard, units),
        "sums_o": (8, width),
        "bias_o": (8, local),
    }
    chain = (2, n - 1, rows, width)
    buffers = {
        "x": ((rows, width), F32),
        "cot": ((rows, width), F32),
        "xr": ((n, rows, width), BF),
        "dr": ((n, rows, width), BF),
        "qkv": ((dp, 3, shard, local), BF),
        "pj": ((dp, shard, local), BF),
        "pv": ((local, shard), BF),
        "dv": ((units, shard), BF),
        "ud": ((2, dp, 2, shard, units), BF),
        "qvb": ((2, local), F32),
        "bb": ((2, width), F32),
        "ub": ((2, 1, units), F32),
        "gain": ((2, width), F32),
        "nb": ((2, width), F32),
        "q": ((seq, local), BF),
        "k": ((seq, local), BF),
        "v": ((seq, local), BF),
        "ctx": ((seq, local), BF),
        "dctx": ((seq, local), BF),
        "dm": ((3, seq, local), BF),
        "prob": ((heads, seq, seq), F32),
        "terms": ((n, rows, width), F32),
        "s1": (chain, BF),
        "r1": (chain, BF),
        "s2": (chain, BF),
        "r2": (chain, BF),
        "acc": ((rows, width), F32),
        "n1": ((rows, width), F32),
        "i1": ((rows, 1), F32),
        "mid": ((rows, width), F32),
        "dres": ((rows, width), F32),
        "m_all": ((2, rows, width), BF),
        "d_all": ((2, rows, width), BF),
        "pre": ((2, rows, 2 * units), F32),
        "act": ((2, rows, 2 * units), BF),
        "dpre": ((2, rows, 2 * units), BF),
        "ps": ((2, rows, width), BF),
        "pr": ((2, rows, width), BF),
        "g": ((2, dp, 2, shard, units), BF),
        "gp": ((2, chips, 2, shard, units), BF),
        "gs": ((2, chips, 2, shard, units), BF),
        "gl": ((2, chips, 2, shard, units), BF),
        "zs": ((2, shard, units), BF),
        "zr": ((2, shard, units), BF),
        "a": ((dp, 4, shard, local), BF),
        "ap": ((chips, 4, shard, local), BF),
        "as_": ((chips, 4, shard, local), BF),
        "al": ((chips, 4, shard, local), BF),
        "sums": ((8, width), F32),
        "sp": ((8, width), F32),
        "sc": ((chips, 8, width), F32),
        "st": ((n, 8, width), F32),
        "b": ((8, local), F32),
        "bp": ((8, local), F32),
        "bc": ((chips, 8, local), F32),
    }
    semaphores = {"lsem": (11,), "m_s": (2,), "m_r": (2,), "z_s": (4,), "z_r": (4,)}
    for name, shape in {
        "xg": (2, n - 1, CH),
        "dg": (2, n - 1, CH),
        "r1": (2, n - 1, CH),
        "r2": (2, n - 1, CH),
        "w": (4, 2 * chips),
        "p": (4, CH),
        "gc": (2, chips),
        "gx": (2, chips),
        "ac": (chips,),
        "ax": (chips,),
        "sc": (chips,),
        "bc": (chips,),
        "st": (n,),
    }.items():
        semaphores[name + "_s"] = shape
        semaphores[name + "_r"] = shape
    names = list(operands) + list(outs) + list(buffers) + list(semaphores)

    vmem = pl.BlockSpec(memory_space=pltpu.VMEM)
    any_space = pl.BlockSpec(memory_space=pl.ANY)
    results = pl.pallas_call(
        functools.partial(layer_kernel, n, dp, names),
        out_shape=[jax.ShapeDtypeStruct(shape, F32) for shape in outs.values()],
        in_specs=[pl.BlockSpec(memory_space=pltpu.SMEM)] + [any_space] * (len(operands) - 1),
        out_specs=[vmem] * len(outs),
        scratch_shapes=[pltpu.VMEM(shape, kind) for shape, kind in buffers.values()]
        + [dma(shape) for shape in semaphores.values()],
        compiler_params=pltpu.CompilerParams(
            collective_id=0, has_side_effects=True, vmem_limit_bytes=56 * 2**20
        ),
    )(*operands.values())
    finals = [
        (rows, width),
        (rows, width),
        (3, shard, local),
        (2, local),
        (local, shard),
        (2, width),
        (shard, units),
        (1, units),
        (units, shard),
        (2, width),
        (2, width),
    ]
    hidden, dx, qkv, qvb, proj, branch, up, ub, down, gain, nb = pl.pallas_call(
        store_kernel,
        out_shape=[jax.ShapeDtypeStruct(shape, F32) for shape in finals],
        in_specs=[vmem] * len(outs),
        out_specs=[vmem] * len(finals),
    )(*results)
    return (
        hidden,
        dx,
        qkv[None],
        qvb[None],
        proj[None],
        branch[None],
        up[None],
        ub,
        down[None],
        gain[None],
        nb[None],
    )


def solution(mesh):
    placed = (
        P(("dp", "tensor"), None),
        P("dp"),
        P(None, None, "dp", "tensor"),
        P(None, None, "tensor"),
        P(None, "tensor", "dp"),
        P(),
        P(None, "dp", "tensor"),
        P(None, "tensor"),
        P(None, "tensor", "dp"),
        P(),
        P(),
        P(("dp", "tensor"), None),
    )
    return jax.shard_map(
        per_device,
        mesh=mesh,
        in_specs=placed,
        out_specs=(
            P(("dp", "tensor"), None),
            P(("dp", "tensor"), None),
            P(None, None, "dp", "tensor"),
            P(None, None, "tensor"),
            P(None, "tensor", "dp"),
            P(),
            P(None, "dp", "tensor"),
            P(None, "tensor"),
            P(None, "tensor", "dp"),
            P(),
            P(),
        ),
        check_vma=False,
    )
```

```python
import functools
import math
from types import SimpleNamespace

import jax
import jax.numpy as jnp
from jax import lax
from jax.experimental import pallas as pl
from jax.experimental.pallas import tpu as pltpu
from jax.sharding import PartitionSpec as P

MESH = pl.DeviceIdType.MESH
BF = jnp.bfloat16
F32 = jnp.float32
HD = 64
CH = 2

norm_eps = 1e-12
half_root = 0.7071067811865476
inv_root = 0.3989422804014327


def layer_norm(residual):
    centred = residual - jnp.mean(residual, axis=-1, keepdims=True)
    inverse = lax.rsqrt(jnp.mean(centred * centred, axis=-1, keepdims=True) + norm_eps)
    return (centred * inverse, inverse)


def norm_back(upstream, normed, inverse, gain_row):
    scaled = upstream * gain_row
    return inverse * (
        scaled
        - jnp.mean(scaled, axis=-1, keepdims=True)
        - normed * jnp.mean(scaled * normed, axis=-1, keepdims=True)
    )


def gelu_value(pre_act):
    return 0.5 * pre_act * (1.0 + lax.erf(pre_act * half_root))


def gelu_slope(pre_act):
    return (
        0.5 * (1.0 + lax.erf(pre_act * half_root))
        + pre_act * jnp.exp(-0.5 * pre_act * pre_act) * inv_root
    )


def nn_dot(left, right):
    return jnp.dot(left, right, preferred_element_type=F32)


def nt_dot(left, right):
    return lax.dot_general(left, right, (((1,), (1,)), ((), ())), preferred_element_type=F32)


def tn_dot(left, right):
    return lax.dot_general(left, right, (((0,), (0,)), ((), ())), preferred_element_type=F32)


def turned(block):
    size = block.shape[1]
    row = lax.broadcasted_iota(jnp.int32, (size, size), 0)
    col = lax.broadcasted_iota(jnp.int32, (size, size), 1)
    return nt_dot(jnp.where(row == col, 1.0, 0.0).astype(BF), block).astype(BF)


def send(src, dst, send_sem, recv_sem, axis, target):
    return pltpu.make_async_remote_copy(
        src_ref=src,
        dst_ref=dst,
        send_sem=send_sem,
        recv_sem=recv_sem,
        device_id={axis: target},
        device_id_type=MESH,
    )


def ways(me, n):
    return ((0, me, me + 1), (1, n - 1 - me, me - 1))


class ChainGather:
    def __init__(self, buf, me, n, ssem, rsem):
        self.buf, self.me, self.n, self.ssem, self.rsem = buf, me, n, ssem, rsem
        self.chunk = buf.shape[1] // CH

    def link(self, way, s, c, pos, target):
        block = pos - s
        block = block if way == 0 else self.n - 1 - block
        view = self.buf.at[block, pl.ds(c * self.chunk, self.chunk)]
        sems = self.ssem.at[way, s, c], self.rsem.at[way, s, c]
        return send(view, view, *sems, "tensor", target)

    def step(self, s, c):
        for way, pos, target in ways(self.me, self.n):

            @pl.when(jnp.logical_and(pos >= s, pos < self.n - 1))
            def _(way=way, pos=pos, target=target):
                if s > 0:
                    self.link(way, s - 1, c, pos - 1, target).wait_recv()
                self.link(way, s, c, pos, target).start()

    def steps(self, s):
        for c in range(CH):
            self.step(s, c)

    def last(self):
        for way, pos, target in ways(self.me, self.n):

            @pl.when(pos == self.n - 1)
            def _(way=way, pos=pos, target=target):
                for s in range(self.n - 1):
                    for c in range(CH):
                        self.link(way, s, c, pos - 1, target).wait_recv()

    def finish(self):
        for s in range(self.n - 1):
            for way, pos, target in ways(self.me, self.n):

                @pl.when(jnp.logical_and(pos >= s, pos < self.n - 1))
                def _(way=way, pos=pos, target=target):
                    for c in range(CH):
                        self.link(way, s, c, pos, target).wait_send()


class ChainReduce:
    def __init__(self, terms, me, n, sbuf, rbuf, ssem, rsem):
        self.terms, self.me, self.n = terms, me, n
        self.sbuf, self.rbuf, self.ssem, self.rsem = sbuf, rbuf, ssem, rsem
        self.chunk = terms.shape[1] // CH

    def part(self, c):
        return pl.ds(c * self.chunk, self.chunk)

    def link(self, way, s, c, target):
        return send(
            self.sbuf.at[way, s, self.part(c)],
            self.rbuf.at[way, s, self.part(c)],
            self.ssem.at[way, s, c],
            self.rsem.at[way, s, c],
            "tensor",
            target,
        )

    def step(self, s, c):
        for way, pos, target in ways(self.me, self.n):
            owner = self.n - 1 - s + pos
            block = owner if way == 0 else self.n - 1 - owner

            @pl.when(pos <= s)
            def _(way=way, pos=pos, target=target, block=block):
                if s == 0:
                    self.sbuf[way, s, self.part(c)] = self.terms[block, self.part(c)].astype(BF)
                else:

                    @pl.when(pos == 0)
                    def _():
                        self.sbuf[way, s, self.part(c)] = self.terms[block, self.part(c)].astype(BF)

                    @pl.when(pos > 0)
                    def _():
                        self.link(way, s - 1, c, target).wait_recv()
                        got = self.rbuf[way, s - 1, self.part(c)].astype(F32)
                        self.sbuf[way, s, self.part(c)] = (
                            self.terms[block, self.part(c)] + got
                        ).astype(BF)

                self.link(way, s, c, target).start()

    def steps(self, s):
        for c in range(CH):
            self.step(s, c)

    def total(self, c, acc):
        acc[self.part(c)] = self.terms[self.me, self.part(c)]
        for way, pos, target in ways(self.me, self.n):

            @pl.when(pos > 0)
            def _(way=way, target=target):
                self.link(way, self.n - 2, c, target).wait_recv()
                acc[self.part(c)] += self.rbuf[way, self.n - 2, self.part(c)].astype(F32)

    def finish(self):
        for s in range(self.n - 1):
            for way, pos, target in ways(self.me, self.n):

                @pl.when(pos <= s)
                def _(way=way, target=target):
                    for c in range(CH):
                        self.link(way, s, c, target).wait_send()


class Plane:
    def __init__(self, mine, dp, way):
        chips = dp // 2
        chip = lax.div(mine, 2)
        self.core_index = lax.rem(mine, 2)
        self.mate = mine + 1 - 2 * self.core_index
        self.way = way
        if way == 0:
            self.first, self.second = chips, 1
            self.f, self.g = chip, 0
        elif way == 1:
            self.first, self.second = 2, chips // 2
            self.f, self.g = lax.rem(chip, 2), lax.div(chip, 2)
        else:
            self.first, self.second = chips // 2, 2
            self.f, self.g = lax.div(chip, 2), lax.rem(chip, 2)
        self.spots = [(i, j) for j in range(self.second) for i in range(self.first)]

    def at(self, i, j, other_core=False):
        f = lax.rem(self.f + i % self.first, self.first)
        g = lax.rem(self.g + j % self.second, self.second) if self.second > 1 else 0
        chip = f if self.way == 0 else (2 * g + f if self.way == 1 else 2 * f + g)
        return 2 * chip + (1 - self.core_index if other_core else self.core_index)

    def slot(self, i, j):
        return i * self.second + j


class PlaneGather:
    def __init__(self, buf, grid, ssem, rsem):
        self.buf, self.grid, self.ssem, self.rsem = buf, grid, ssem, rsem
        self.chips = grid.first * grid.second

    def chip(self, i, j):
        k = self.grid.slot(i, j) - 1
        sems = self.ssem.at[k], self.rsem.at[k]
        if j == 0:
            view, target = self.buf.at[self.grid.at(0, 0)], self.grid.at(i, 0)
        else:
            view, target = self.buf.at[self.grid.at(-i, 0)], self.grid.at(0, j)
        return send(view, view, *sems, "dp", target)

    def core(self, i, j):
        view = self.buf.at[self.grid.at(-i, -j)]
        k = self.chips - 1 + self.grid.slot(i, j)
        return send(view, view, self.ssem.at[k], self.rsem.at[k], "dp", self.grid.mate)

    def start(self):
        for i in range(1, self.grid.first):
            self.chip(i, 0).start()
        for j in range(1, self.grid.second):
            self.chip(0, j).start()
        self.core(0, 0).start()

    def relay(self):
        for i in range(1, self.grid.first):
            self.chip(i, 0).wait_recv()
            for j in range(1, self.grid.second):
                self.chip(i, j).start()
            self.core(i, 0).start()

    def relay_rest(self):
        for i, j in self.grid.spots:
            if j > 0:
                self.chip(i, j).wait_recv()
                self.core(i, j).start()

    def last(self):
        for i, j in self.grid.spots:
            self.core(i, j).wait_recv()

    def finish(self):
        for i, j in self.grid.spots:
            if i > 0 or j > 0:
                self.chip(i, j).wait_send()
            self.core(i, j).wait_send()


class PlaneReduce:
    def __init__(self, parts, got, summed, land, grid, sems):
        self.parts, self.got, self.summed, self.land = parts, got, summed, land
        self.grid, self.sems = grid, sems

    def core(self):
        grid = self.grid
        part = self.parts.at[1 - grid.core_index]
        return send(part, self.got, self.sems[0], self.sems[1], "dp", grid.mate)

    def chip(self, i, j):
        k = self.grid.slot(i, j)
        target = self.grid.at(-i, 0) if j == 0 else self.grid.at(0, j)
        sems = self.sems[2].at[k - 1], self.sems[3].at[k - 1]
        return send(self.summed.at[k], self.land.at[k], *sems, "dp", target)

    def start(self):
        self.core().start()

    def pair(self, i, j):
        spot = lax.div(self.grid.at(-i, j), 2)
        return self.parts[self.grid.core_index, spot].astype(F32) + self.got[spot].astype(F32)

    def spread(self):
        self.core().wait_recv()
        for i, j in reversed(self.grid.spots):
            if j > 0:
                self.summed[self.grid.slot(i, j)] = self.pair(i, j).astype(BF)
                self.chip(i, j).start()

    def row(self, i):
        total = self.pair(i, 0)
        for j in range(1, self.grid.second):
            self.chip(i, j).wait_recv()
            total = total + self.land[self.grid.slot(i, j)].astype(F32)
        return total

    def spread_rest(self):
        for i in range(1, self.grid.first):
            self.summed[self.grid.slot(i, 0)] = self.row(i).astype(BF)
            self.chip(i, 0).start()

    def total(self):
        total = self.row(0)
        for i in range(1, self.grid.first):
            self.chip(i, 0).wait_recv()
            total = total + self.land[self.grid.slot(i, 0)].astype(F32)
        return total

    def finish(self):
        self.core().wait_send()
        for i, j in self.grid.spots:
            if i > 0 or j > 0:
                self.chip(i, j).wait_send()


def joined(value):
    parts, rows, columns = value.shape
    if rows % 16 == 0:
        return value.reshape(parts * rows, columns)
    return jnp.concatenate([value[d] for d in range(parts)], axis=0)


def put_parts(ref, value, *where):
    chips, rows = ref.shape[1], ref.shape[-2]
    for d in range(2 * chips):
        ref[(d % 2, d // 2) + where] = value[d * rows : (d + 1) * rows].astype(BF)


def layer_kernel(n, dp, names, *refs):
    r = SimpleNamespace(**dict(zip(names, refs)))
    me = lax.axis_index("tensor")
    mine = lax.axis_index("dp")
    chips = dp // 2
    chip = lax.div(mine, 2)
    core_mate = mine + 1 - 2 * lax.rem(mine, 2)
    pair_mate = me + 1 - 2 * lax.rem(me, 2)
    far = lax.rem(me + n // 2, n)
    own_rows, width = r.x.shape
    local = r.q.shape[1]
    units = r.ub.shape[-1]
    chunk = own_rows // CH
    scale = 1.0 / math.sqrt(HD)

    loads = {
        name: pltpu.make_async_copy(src, dst, r.lsem.at[k])
        for k, (name, src, dst) in enumerate(
            [
                ("x", r.x_h, r.x),
                ("qkv", r.qkv_h, r.aw.at[mine, pl.ds(0, 3)]),
                ("proj", r.proj_h, r.pv),
                ("down", r.down_h, r.ud.at[mine, 1]),
                ("up", r.up_h, r.ud.at[mine, 0]),
                ("ub", r.ub_h, r.ub.at[0]),
                ("qvb", r.qvb_h, r.qvb),
                ("bb", r.bb_h, r.bb),
                ("gain", r.gain_h, r.gain),
                ("nb", r.nb_h, r.nb),
                ("cot", r.cot_h, r.cot),
            ]
        )
    }
    for copy in loads.values():
        copy.start()
    stores = {
        name: pltpu.make_async_copy(src, getattr(r, name + "_o"), r.lsem.at[k])
        for k, (name, src) in enumerate(
            [
                ("hidden", r.hidden),
                ("dx", r.acc),
                ("qkv", r.qkvg),
                ("qvb", r.qvbg),
                ("proj", r.projg),
                ("branch", r.branchg),
                ("up", r.ffg.at[0]),
                ("ub", r.ubg),
                ("down", r.ffg.at[1]),
                ("gain", r.gaing),
                ("nb", r.nbg),
            ]
        )
    }

    barrier = pltpu.get_barrier_semaphore()
    for k in range(1, n):
        pl.semaphore_signal(
            barrier, inc=1, device_id={"tensor": lax.rem(me + k, n)}, device_id_type=MESH
        )
    for k in range(1, chips):
        pl.semaphore_signal(
            barrier, inc=1, device_id={"dp": lax.rem(mine + 2 * k, dp)}, device_id_type=MESH
        )
    pl.semaphore_signal(barrier, inc=1, device_id={"dp": core_mate}, device_id_type=MESH)

    loads["x"].wait()
    r.xr[me] = r.x[...].astype(BF)
    loads["proj"].wait()
    r.aw[mine, 3] = turned(r.pv[...])
    for name in ("qkv", "up", "down", "ub"):
        loads[name].wait()
    pl.semaphore_wait(barrier, n - 1 + chips)

    xg = ChainGather(r.xr, me, n, r.xg_s, r.xg_r)
    grids = [Plane(mine, dp, way) for way in range(3)]
    gathers = [
        PlaneGather(buf, grids[way], r.w_s.at[k], r.w_r.at[k])
        for k, (buf, way) in enumerate(((r.aw, 0), (r.ud, 1), (r.fu, 2), (r.fd, 2)))
    ]
    inner = jnp.logical_and(me > 0, me < n - 1)
    g_attn, g_ud, g_far_up, g_far_down = gathers

    def far_copy(k):
        src, dst = (
            (r.ud.at[mine, 0], r.fu.at[mine]),
            (r.ud.at[mine, 1], r.fd.at[mine]),
            (r.ub.at[0], r.ub.at[1]),
            (r.zs.at[0], r.zr.at[0]),
            (r.zs.at[1], r.zr.at[1]),
        )[k]
        return send(src, dst, r.z_s.at[k], r.z_r.at[k], "tensor", far)

    def pair_copy(phase, c, src, dst):
        return send(
            src.at[pl.ds(c * chunk, chunk)],
            dst.at[pl.ds(c * chunk, chunk)],
            r.p_s.at[phase % 2, c],
            r.p_r.at[phase % 2, c],
            "tensor",
            pair_mate,
        )

    def rows_of(c):
        return pl.ds(c * chunk, chunk)

    xg.steps(0)
    g_attn.start()
    g_ud.start()
    xg.steps(1)
    xg.steps(2)
    g_attn.relay()
    @pl.when(jnp.logical_not(inner))
    def _():
        for k in range(3):
            far_copy(k).start()

    for name in ("qvb", "bb", "gain", "nb", "cot"):
        loads[name].wait()
    g_attn.last()
    xg.last()

    rounded = joined(r.xr[...])
    r.q[...] = (nn_dot(rounded, joined(r.aw[:, 0])) + r.qvb[0:1, :]).astype(BF)
    r.k[...] = nn_dot(rounded, joined(r.aw[:, 1])).astype(BF)
    r.v[...] = (nn_dot(rounded, joined(r.aw[:, 2])) + r.qvb[1:2, :]).astype(BF)
    seq_rows = r.q.shape[0]
    valid = lax.broadcasted_iota(jnp.int32, (seq_rows, seq_rows), 1) < r.lengths[0]
    heads = local // HD
    for head in range(heads):
        cols = slice(head * HD, (head + 1) * HD)
        scores = jnp.where(valid, nt_dot(r.q[:, cols], r.k[:, cols]) * scale, -1e30)
        weights = jnp.exp(scores - jnp.max(scores, axis=-1, keepdims=True))
        prob = weights * (1.0 / jnp.sum(weights, axis=-1, keepdims=True))
        r.prob[head] = prob
        r.ctx[:, cols] = nn_dot(prob.astype(BF), r.v[:, cols]).astype(BF)
    @pl.when(inner)
    def _():
        for k in range(3):
            far_copy(k).start()

    r.terms[...] = nt_dot(r.ctx[...], joined(r.aw[:, 3])).reshape(r.terms.shape)

    red = ChainReduce(r.terms, me, n, r.s1, r.r1, r.r1_s, r.r1_r)
    red.steps(0)
    g_ud.relay()
    far_copy(0).wait_recv()
    g_far_up.start()
    red.steps(1)
    far_copy(1).wait_recv()
    g_far_down.start()
    g_ud.relay_rest()
    red.steps(2)
    g_far_up.relay()
    for c in range(CH):
        part = rows_of(c)
        red.total(c, r.acc)
        normed, inverse = layer_norm(r.x[part] + r.acc[part] + r.bb[0:1, :])
        middle = normed * r.gain[0:1, :] + r.nb[0:1, :]
        r.n1[part] = normed
        r.i1[part] = inverse
        r.mid[part] = middle
        r.m_all[0, part] = middle.astype(BF)
        pair_copy(0, c, r.m_all.at[0], r.m_all.at[1]).start()
    g_ud.last()
    g_far_down.relay()
    g_far_up.relay_rest()
    far_copy(2).wait_recv()

    def up_of(h):
        return r.ud[:, 0] if h == 0 else r.fu[...]

    def down_of(h):
        return r.ud[:, 1] if h == 0 else r.fd[...]

    every = slice(0, own_rows)
    halves = [slice(c * chunk, (c + 1) * chunk) for c in range(CH)]

    def up_rows(group, h, part):
        cols = slice(h * units, (h + 1) * units)
        pre = nn_dot(r.m_all[group, part], joined(up_of(h))) + r.ub[h]
        r.pre[group, part, cols] = pre
        r.act[group, part, cols] = gelu_value(pre).astype(BF)

    def down_rows(group, part):
        return nt_dot(r.act[group, part, :units], joined(down_of(0))) + nt_dot(
            r.act[group, part, units:], joined(down_of(1))
        )

    up_rows(0, 0, every)
    g_far_up.last()
    up_rows(0, 1, every)
    g_far_down.relay_rest()
    for c, part in enumerate(halves):
        pair_copy(0, c, r.m_all.at[0], r.m_all.at[1]).wait_recv()
        up_rows(1, 0, part)
        up_rows(1, 1, part)
        if c == 0:
            g_far_down.last()
        r.ps[0, part] = down_rows(1, part).astype(BF)
        pair_copy(1, c, r.ps.at[0], r.pr.at[0]).start()
    r.acc[...] = down_rows(0, every)
    for group in range(2):
        for h in range(2):
            cols = slice(h * units, (h + 1) * units)
            r.pre[group, :, cols] = gelu_slope(r.pre[group, :, cols])

    for c in range(CH):
        part = rows_of(c)
        pair_copy(1, c, r.ps.at[0], r.pr.at[0]).wait_recv()
        normed, inverse = layer_norm(
            r.mid[part] + r.acc[part] + r.pr[0, part].astype(F32) + r.bb[1:2, :]
        )
        dres = norm_back(r.cot[part], normed, inverse, r.gain[1:2, :])
        r.d_all[0, part] = dres.astype(BF)
        pair_copy(0, c, r.m_all.at[0], r.m_all.at[1]).wait_send()
        pair_copy(2, c, r.d_all.at[0], r.d_all.at[1]).start()
        r.dres[part] = dres
        r.acc[part] = normed
    r.hidden[...] = r.acc[...] * r.gain[1:2, :] + r.nb[1:2, :]
    stores["hidden"].start()
    r.sums[3:4, :] = jnp.sum(r.cot[...] * r.acc[...], axis=0, keepdims=True)
    r.sums[4:5, :] = jnp.sum(r.cot[...], axis=0, keepdims=True)
    r.sums[5:6, :] = jnp.sum(r.dres[...], axis=0, keepdims=True)

    def back_rows(group, h, part):
        cols = slice(h * units, (h + 1) * units)
        dpre = nn_dot(r.d_all[group, part], joined(down_of(h))) * r.pre[group, part, cols]
        r.dpre[group, part, cols] = dpre.astype(BF)
        total = jnp.sum(dpre, axis=0, keepdims=True)
        r.sums[6 + h : 7 + h, :] = total if group == 0 else r.sums[6 + h : 7 + h, :] + total

    def up_back(group, part):
        return nt_dot(r.dpre[group, part, :units], joined(up_of(0))) + nt_dot(
            r.dpre[group, part, units:], joined(up_of(1))
        )

    back_rows(0, 0, every)
    back_rows(0, 1, every)
    for c, part in enumerate(halves):
        pair_copy(2, c, r.d_all.at[0], r.d_all.at[1]).wait_recv()
        back_rows(1, 0, part)
        back_rows(1, 1, part)
        r.ps[1, part] = up_back(1, part).astype(BF)
        pair_copy(1, c, r.ps.at[0], r.pr.at[0]).wait_send()
        pair_copy(3, c, r.ps.at[1], r.pr.at[1]).start()
    xg.finish()
    red.finish()
    reduces = {
        (h, t): PlaneReduce(
            r.g.at[h, t], r.gp.at[h, t], r.gs.at[h, t], r.gl.at[h, t], grids[1 + t],
            [sem.at[2 * h + t] for sem in (r.gc_s, r.gc_r, r.gx_s, r.gx_r)],
        )
        for h in range(2)
        for t in range(2)
    }

    def weight_part(h, t):
        cols = slice(h * units, (h + 1) * units)
        if t == 0:
            left, right = r.m_all[...], r.dpre[:, :, cols]
        else:
            left, right = r.d_all[...], r.act[:, :, cols]
        put_parts(r.g.at[h, t], tn_dot(joined(left), joined(right)))
        reduces[h, t].start()

    weight_part(1, 1)
    weight_part(1, 0)
    r.acc[...] = up_back(0, every) + r.dres[...]
    reduces[1, 1].spread()
    weight_part(0, 1)
    weight_part(0, 0)
    dg = ChainGather(r.dr, me, n, r.xg_s, r.xg_r)
    for c in range(CH):
        part = rows_of(c)
        pair_copy(3, c, r.ps.at[1], r.pr.at[1]).wait_recv()
        dmid = r.acc[part] + r.pr[1, part].astype(F32)
        dres = norm_back(dmid, r.n1[part], r.i1[part], r.gain[0:1, :])
        r.dr[me, part] = dres.astype(BF)
        dg.step(0, c)
        r.acc[part] = dmid
        r.dres[part] = dres
    reduces[1, 0].spread()
    r.sums[0:1, :] = jnp.sum(r.acc[...] * r.n1[...], axis=0, keepdims=True)
    r.sums[1:2, :] = jnp.sum(r.acc[...], axis=0, keepdims=True)
    r.sums[2:3, :] = jnp.sum(r.dres[...], axis=0, keepdims=True)

    def sum_mate():
        return send(r.sums, r.sp, r.m_s.at[0], r.m_r.at[0], "dp", core_mate)

    def bias_mate():
        return send(r.b, r.bp, r.m_s.at[1], r.m_r.at[1], "dp", core_mate)

    def bias_chip(k):
        view = r.bc.at[chip]
        sems = r.bc_s.at[k - 1], r.bc_r.at[k - 1]
        return send(view, view, *sems, "dp", lax.rem(mine + 2 * k, dp))

    def sum_chip(k):
        view = r.sc.at[chip]
        sems = r.sc_s.at[k - 1], r.sc_r.at[k - 1]
        return send(view, view, *sems, "dp", lax.rem(mine + 2 * k, dp))

    def sum_z(k):
        view = r.st.at[me]
        return send(view, view, r.st_s.at[k - 1], r.st_r.at[k - 1], "tensor", lax.rem(me + k, n))

    sum_mate().start()
    dg.steps(1)
    sum_mate().wait_recv()
    r.sc[chip] = r.sums[...] + r.sp[...]
    for k in range(1, chips):
        sum_chip(k).start()
    reduces[1, 1].spread_rest()
    dg.steps(2)
    reduces[1, 0].spread_rest()
    reduces[0, 1].spread()
    reduces[0, 0].spread()
    for t in (1, 0):
        r.zs[t] = reduces[1, t].total().astype(BF)

    @pl.when(jnp.logical_not(inner))
    def _():
        far_copy(4).start()
        far_copy(3).start()

    dg.last()

    for k in range(1, chips):
        sum_chip(k).wait_recv()
    total = r.sc[0]
    for k in range(1, chips):
        total = total + r.sc[k]
    r.st[me] = total
    for k in range(1, n):
        sum_z(k).start()
    dres_all = joined(r.dr[...])
    r.dctx[...] = nn_dot(dres_all, joined(r.aw[:, 3])).astype(BF)
    r.b[...] = jnp.zeros_like(r.b)
    for head in range(heads):
        cols = slice(head * HD, (head + 1) * HD)
        prob = r.prob[head]
        dc = r.dctx[:, cols]
        dprob = nt_dot(dc, r.v[:, cols])
        weighted = jnp.sum(prob * dprob, axis=-1, keepdims=True)
        dscore = (prob * (dprob - weighted) * scale).astype(BF)
        dquery = nn_dot(dscore, r.k[:, cols])
        dvalue = tn_dot(prob.astype(BF), dc)
        r.dm[0, :, cols] = dquery.astype(BF)
        r.dm[1, :, cols] = tn_dot(dscore, r.q[:, cols]).astype(BF)
        r.dm[2, :, cols] = dvalue.astype(BF)
        r.b[0:1, cols] = jnp.sum(dquery, axis=0, keepdims=True)
        r.b[1:2, cols] = jnp.sum(dvalue, axis=0, keepdims=True)
    bias_mate().start()
    @pl.when(inner)
    def _():
        far_copy(4).start()
        far_copy(3).start()

    dx = nt_dot(r.dm[0], joined(r.aw[:, 0]))
    for j in range(1, 3):
        dx = dx + nt_dot(r.dm[j], joined(r.aw[:, j]))
    r.terms[...] = dx.reshape(r.terms.shape)

    red_x = ChainReduce(r.terms, me, n, r.s2, r.r2, r.r1_s, r.r1_r)
    red_x.steps(0)
    bias_mate().wait_recv()
    r.bc[chip] = r.b[...] + r.bp[...]
    for k in range(1, chips):
        bias_chip(k).start()
    reduces[0, 1].spread_rest()
    reduces[0, 0].spread_rest()
    attn = PlaneReduce(
        r.a, r.ap, r.as_, r.al, grids[0], (r.ac_s, r.ac_r, r.ax_s, r.ax_r)
    )
    rounded = joined(r.xr[...])
    for j in range(3):
        put_parts(r.a, tn_dot(rounded, r.dm[j]), j)
    put_parts(r.a, tn_dot(joined(r.dr[...]), r.ctx[...]), 3)
    attn.start()
    red_x.steps(1)
    attn.spread()
    attn.spread_rest()
    red_x.steps(2)

    for k in range(1, n):
        sum_z(k).wait_recv()
    total = r.st[0]
    for k in range(1, n):
        total = total + r.st[k]
    for j in range(2):
        for k, ref in enumerate((r.gaing, r.nbg, r.branchg)):
            ref[j : j + 1, :] = total[3 * j + k : 3 * j + k + 1]
    r.ubg[...] = r.st[me, 6:7] + r.st[far, 7:8]
    for k in range(1, chips):
        bias_chip(k).wait_recv()
    total = r.bc[0]
    for k in range(1, chips):
        total = total + r.bc[k]
    r.qvbg[...] = total[0:2]
    for name in ("gain", "nb", "branch", "ub", "qvb"):
        stores[name].start()
    for c in range(CH):
        red_x.total(c, r.acc)
    r.acc[...] += r.dres[...]
    stores["dx"].start()
    for t in range(2):
        r.ffg[t] = reduces[0, t].total()
    for t in (1, 0):
        far_copy(3 + t).wait_recv()
        r.ffg[t] += r.zr[t].astype(F32)
    stores["up"].start()
    stores["down"].start()
    total = attn.total()
    r.qkvg[...] = total[0:3]
    r.projg[...] = total[3].T
    stores["qkv"].start()
    stores["proj"].start()

    dg.finish()
    red_x.finish()
    for gather in gathers:
        gather.finish()
    for reduce in list(reduces.values()) + [attn]:
        reduce.finish()
    for k in range(5):
        far_copy(k).wait_send()
    for c in range(CH):
        pair_copy(2, c, r.d_all.at[0], r.d_all.at[1]).wait_send()
        pair_copy(3, c, r.ps.at[1], r.pr.at[1]).wait_send()
    sum_mate().wait_send()
    bias_mate().wait_send()
    for k in range(1, chips):
        sum_chip(k).wait_send()
        bias_chip(k).wait_send()
    for k in range(1, n):
        sum_z(k).wait_send()
    for copy in stores.values():
        copy.wait()


def store_kernel(count, *refs):
    for k in range(count):
        refs[count + k][...] = refs[k][...]


def per_device(
    inputs,
    lengths,
    qkv_weight,
    qv_bias,
    proj_weight,
    branch_bias,
    up_weight,
    up_bias,
    down_weight,
    norm_gain,
    norm_bias,
    cotangent,
):
    n = lax.axis_size("tensor")
    dp = lax.axis_size("dp")
    rows, width = inputs.shape
    shard, local = qkv_weight.shape[2:]
    units = up_weight.shape[2]
    chips = dp // 2
    seq = rows * n
    heads = local // HD
    dma = pltpu.SemaphoreType.DMA

    operands = {
        "lengths": lengths,
        "x_h": inputs,
        "qkv_h": qkv_weight[0],
        "qvb_h": qv_bias[0],
        "proj_h": proj_weight[0],
        "bb_h": branch_bias[0],
        "up_h": up_weight[0],
        "ub_h": up_bias,
        "down_h": down_weight[0].T,
        "gain_h": norm_gain[0],
        "nb_h": norm_bias[0],
        "cot_h": cotangent,
    }
    outs = {
        "hidden_o": (rows, width),
        "dx_o": (rows, width),
        "qkv_o": (3, shard, local),
        "qvb_o": (2, local),
        "proj_o": (local, shard),
        "branch_o": (2, width),
        "up_o": (shard, units),
        "ub_o": (1, units),
        "down_o": (shard, units),
        "gain_o": (2, width),
        "nb_o": (2, width),
    }
    chain = (2, n - 1, rows, width)
    buffers = {
        "x": ((rows, width), F32),
        "cot": ((rows, width), F32),
        "xr": ((n, rows, width), BF),
        "dr": ((n, rows, width), BF),
        "aw": ((dp, 4, shard, local), BF),
        "pv": ((local, shard), BF),
        "ud": ((dp, 2, shard, units), BF),
        "fu": ((dp, shard, units), BF),
        "fd": ((dp, shard, units), BF),
        "qvb": ((2, local), F32),
        "bb": ((2, width), F32),
        "ub": ((2, 1, units), F32),
        "gain": ((2, width), F32),
        "nb": ((2, width), F32),
        "q": ((seq, local), BF),
        "k": ((seq, local), BF),
        "v": ((seq, local), BF),
        "ctx": ((seq, local), BF),
        "dctx": ((seq, local), BF),
        "dm": ((3, seq, local), BF),
        "prob": ((heads, seq, seq), F32),
        "terms": ((n, rows, width), F32),
        "s1": (chain, BF),
        "r1": (chain, BF),
        "s2": (chain, BF),
        "r2": (chain, BF),
        "acc": ((rows, width), F32),
        "n1": ((rows, width), F32),
        "i1": ((rows, 1), F32),
        "mid": ((rows, width), F32),
        "dres": ((rows, width), F32),
        "m_all": ((2, rows, width), BF),
        "d_all": ((2, rows, width), BF),
        "pre": ((2, rows, 2 * units), F32),
        "act": ((2, rows, 2 * units), BF),
        "dpre": ((2, rows, 2 * units), BF),
        "ps": ((2, rows, width), BF),
        "pr": ((2, rows, width), BF),
        "g": ((2, 2, 2, chips, shard, units), BF),
        "gp": ((2, 2, chips, shard, units), BF),
        "gs": ((2, 2, chips, shard, units), BF),
        "gl": ((2, 2, chips, shard, units), BF),
        "zs": ((2, shard, units), BF),
        "zr": ((2, shard, units), BF),
        "a": ((2, chips, 4, shard, local), BF),
        "ap": ((chips, 4, shard, local), BF),
        "as_": ((chips, 4, shard, local), BF),
        "al": ((chips, 4, shard, local), BF),
        "sums": ((8, width), F32),
        "sp": ((8, width), F32),
        "sc": ((chips, 8, width), F32),
        "st": ((n, 8, width), F32),
        "b": ((8, local), F32),
        "bp": ((8, local), F32),
        "bc": ((chips, 8, local), F32),
        "hidden": ((rows, width), F32),
        "ffg": ((2, shard, units), F32),
        "qkvg": ((3, shard, local), F32),
        "projg": ((local, shard), F32),
        "qvbg": ((2, local), F32),
        "branchg": ((2, width), F32),
        "ubg": ((1, units), F32),
        "gaing": ((2, width), F32),
        "nbg": ((2, width), F32),
    }
    semaphores = {"lsem": (11,)}
    for name, shape in {
        "m": (2,),
        "z": (5,),
        "xg": (2, n - 1, CH),
        "r1": (2, n - 1, CH),
        "w": (4, 2 * chips - 1),
        "p": (2, CH),
        "gc": (4,),
        "gx": (4, chips - 1),
        "ac": (),
        "ax": (chips - 1,),
        "sc": (chips - 1,),
        "bc": (chips - 1,),
        "st": (n - 1,),
    }.items():
        semaphores[name + "_s"] = shape
        semaphores[name + "_r"] = shape
    names = list(operands) + list(outs) + list(buffers) + list(semaphores)

    vmem = pl.BlockSpec(memory_space=pltpu.VMEM)
    any_space = pl.BlockSpec(memory_space=pl.ANY)
    results = pl.pallas_call(
        functools.partial(layer_kernel, n, dp, names),
        out_shape=[jax.ShapeDtypeStruct(shape, F32) for shape in outs.values()],
        in_specs=[pl.BlockSpec(memory_space=pltpu.SMEM)] + [any_space] * (len(operands) - 1),
        out_specs=[any_space] * len(outs),
        scratch_shapes=[pltpu.VMEM(shape, kind) for shape, kind in buffers.values()]
        + [dma(shape) if shape else dma for shape in semaphores.values()],
        compiler_params=pltpu.CompilerParams(
            collective_id=0, has_side_effects=True, vmem_limit_bytes=56 * 2**20
        ),
    )(*operands.values())
    shapes = [jax.ShapeDtypeStruct(shape, F32) for shape in outs.values()]
    hidden, dx, qkv, qvb, proj, branch, up, ub, down, gain, nb = pl.pallas_call(
        functools.partial(store_kernel, len(outs)),
        out_shape=shapes,
        in_specs=[vmem] * len(outs),
        out_specs=[vmem] * len(outs),
    )(*results)
    return (
        hidden,
        dx,
        qkv[None],
        qvb[None],
        proj[None],
        branch[None],
        up[None],
        ub,
        down.T[None],
        gain[None],
        nb[None],
    )


def solution(mesh):
    placed = (
        P(("dp", "tensor"), None),
        P("dp"),
        P(None, None, "dp", "tensor"),
        P(None, None, "tensor"),
        P(None, "tensor", "dp"),
        P(),
        P(None, "dp", "tensor"),
        P(None, "tensor"),
        P(None, "tensor", "dp"),
        P(),
        P(),
        P(("dp", "tensor"), None),
    )
    return jax.shard_map(
        per_device,
        mesh=mesh,
        in_specs=placed,
        out_specs=(
            P(("dp", "tensor"), None),
            P(("dp", "tensor"), None),
            P(None, None, "dp", "tensor"),
            P(None, None, "tensor"),
            P(None, "tensor", "dp"),
            P(),
            P(None, "dp", "tensor"),
            P(None, "tensor"),
            P(None, "tensor", "dp"),
            P(),
            P(),
        ),
        check_vma=False,
    )
```

```python
import functools
import math
from types import SimpleNamespace

import jax
import jax.numpy as jnp
from jax import lax
from jax.experimental import pallas as pl
from jax.experimental.pallas import tpu as pltpu
from jax.sharding import PartitionSpec as P

MESH = pl.DeviceIdType.MESH
BF = jnp.bfloat16
F32 = jnp.float32
HD = 64
CH = 2

norm_eps = 1e-12
half_root = 0.7071067811865476
inv_root = 0.3989422804014327


def layer_norm(residual):
    centred = residual - jnp.mean(residual, axis=-1, keepdims=True)
    inverse = lax.rsqrt(jnp.mean(centred * centred, axis=-1, keepdims=True) + norm_eps)
    return (centred * inverse, inverse)


def norm_back(upstream, normed, inverse, gain_row):
    scaled = upstream * gain_row
    return inverse * (
        scaled
        - jnp.mean(scaled, axis=-1, keepdims=True)
        - normed * jnp.mean(scaled * normed, axis=-1, keepdims=True)
    )


def gelu_value(pre_act):
    return 0.5 * pre_act * (1.0 + lax.erf(pre_act * half_root))


def gelu_slope(pre_act):
    return (
        0.5 * (1.0 + lax.erf(pre_act * half_root))
        + pre_act * jnp.exp(-0.5 * pre_act * pre_act) * inv_root
    )


def nn_dot(left, right):
    return jnp.dot(left, right, preferred_element_type=F32)


def nt_dot(left, right):
    return lax.dot_general(left, right, (((1,), (1,)), ((), ())), preferred_element_type=F32)


def tn_dot(left, right):
    return lax.dot_general(left, right, (((0,), (0,)), ((), ())), preferred_element_type=F32)


def turned(block):
    size = block.shape[1]
    row = lax.broadcasted_iota(jnp.int32, (size, size), 0)
    col = lax.broadcasted_iota(jnp.int32, (size, size), 1)
    return nt_dot(jnp.where(row == col, 1.0, 0.0).astype(BF), block).astype(BF)


def send(src, dst, send_sem, recv_sem, axis, target):
    return pltpu.make_async_remote_copy(
        src_ref=src,
        dst_ref=dst,
        send_sem=send_sem,
        recv_sem=recv_sem,
        device_id={axis: target},
        device_id_type=MESH,
    )


def ways(me, n):
    return ((0, me, me + 1), (1, n - 1 - me, me - 1))


class ChainGather:
    def __init__(self, buf, me, n, ssem, rsem):
        self.buf, self.me, self.n, self.ssem, self.rsem = buf, me, n, ssem, rsem
        self.chunk = buf.shape[1] // CH

    def link(self, way, s, c, pos, target):
        block = pos - s
        block = block if way == 0 else self.n - 1 - block
        view = self.buf.at[block, pl.ds(c * self.chunk, self.chunk)]
        sems = self.ssem.at[way, s, c], self.rsem.at[way, s, c]
        return send(view, view, *sems, "tensor", target)

    def step(self, s, c):
        for way, pos, target in ways(self.me, self.n):

            @pl.when(jnp.logical_and(pos >= s, pos < self.n - 1))
            def _(way=way, pos=pos, target=target):
                if s > 0:
                    self.link(way, s - 1, c, pos - 1, target).wait_recv()
                self.link(way, s, c, pos, target).start()

    def steps(self, s):
        for c in range(CH):
            self.step(s, c)

    def last(self):
        for way, pos, target in ways(self.me, self.n):

            @pl.when(pos == self.n - 1)
            def _(way=way, pos=pos, target=target):
                for s in range(self.n - 1):
                    for c in range(CH):
                        self.link(way, s, c, pos - 1, target).wait_recv()

    def finish(self):
        for s in range(self.n - 1):
            for way, pos, target in ways(self.me, self.n):

                @pl.when(jnp.logical_and(pos >= s, pos < self.n - 1))
                def _(way=way, pos=pos, target=target):
                    for c in range(CH):
                        self.link(way, s, c, pos, target).wait_send()


class ChainReduce:
    def __init__(self, terms, me, n, sbuf, rbuf, ssem, rsem):
        self.terms, self.me, self.n = terms, me, n
        self.sbuf, self.rbuf, self.ssem, self.rsem = sbuf, rbuf, ssem, rsem
        self.chunk = terms.shape[1] // CH

    def part(self, c):
        return pl.ds(c * self.chunk, self.chunk)

    def link(self, way, s, c, target):
        return send(
            self.sbuf.at[way, s, self.part(c)],
            self.rbuf.at[way, s, self.part(c)],
            self.ssem.at[way, s, c],
            self.rsem.at[way, s, c],
            "tensor",
            target,
        )

    def step(self, s, c):
        for way, pos, target in ways(self.me, self.n):
            owner = self.n - 1 - s + pos
            block = owner if way == 0 else self.n - 1 - owner

            @pl.when(pos <= s)
            def _(way=way, pos=pos, target=target, block=block):
                if s == 0:
                    self.sbuf[way, s, self.part(c)] = self.terms[block, self.part(c)].astype(BF)
                else:

                    @pl.when(pos == 0)
                    def _():
                        self.link(way, s - 1, c, target).wait_send()
                        self.sbuf[way, s, self.part(c)] = self.terms[block, self.part(c)].astype(BF)

                    @pl.when(pos > 0)
                    def _():
                        self.link(way, s - 1, c, target).wait_recv()
                        got = self.rbuf[way, s - 1, self.part(c)].astype(F32)
                        self.sbuf[way, s, self.part(c)] = (
                            self.terms[block, self.part(c)] + got
                        ).astype(BF)

                self.link(way, s, c, target).start()

    def steps(self, s):
        for c in range(CH):
            self.step(s, c)

    def total(self, c, acc):
        acc[self.part(c)] = self.terms[self.me, self.part(c)]
        for way, pos, target in ways(self.me, self.n):

            @pl.when(pos > 0)
            def _(way=way, target=target):
                self.link(way, self.n - 2, c, target).wait_recv()
                acc[self.part(c)] += self.rbuf[way, self.n - 2, self.part(c)].astype(F32)

    def finish(self):
        for s in range(self.n - 1):
            for way, pos, target in ways(self.me, self.n):

                @pl.when(jnp.logical_and(pos <= s, jnp.logical_or(pos > 0, s == self.n - 2)))
                def _(way=way, target=target):
                    for c in range(CH):
                        self.link(way, s, c, target).wait_send()


class Plane:
    def __init__(self, mine, dp, way):
        chips = dp // 2
        chip = lax.div(mine, 2)
        self.core_index = lax.rem(mine, 2)
        self.mate = mine + 1 - 2 * self.core_index
        self.way = way
        if way == 0:
            self.first, self.second = chips, 1
            self.f, self.g = chip, 0
        elif way == 1:
            self.first, self.second = 2, chips // 2
            self.f, self.g = lax.rem(chip, 2), lax.div(chip, 2)
        else:
            self.first, self.second = chips // 2, 2
            self.f, self.g = lax.div(chip, 2), lax.rem(chip, 2)
        self.spots = [(i, j) for j in range(self.second) for i in range(self.first)]

    def at(self, i, j, other_core=False):
        f = lax.rem(self.f + i % self.first, self.first)
        g = lax.rem(self.g + j % self.second, self.second) if self.second > 1 else 0
        chip = f if self.way == 0 else (2 * g + f if self.way == 1 else 2 * f + g)
        return 2 * chip + (1 - self.core_index if other_core else self.core_index)

    def slot(self, i, j):
        return i * self.second + j


class PlaneGather:
    def __init__(self, buf, grid, ssem, rsem):
        self.buf, self.grid, self.ssem, self.rsem = buf, grid, ssem, rsem
        self.chips = grid.first * grid.second

    def chip(self, i, j):
        k = self.grid.slot(i, j) - 1
        sems = self.ssem.at[k], self.rsem.at[k]
        if j == 0:
            view, target = self.buf.at[self.grid.at(0, 0)], self.grid.at(i, 0)
        else:
            view, target = self.buf.at[self.grid.at(-i, 0)], self.grid.at(0, j)
        return send(view, view, *sems, "dp", target)

    def core(self, i, j):
        view = self.buf.at[self.grid.at(-i, -j)]
        k = self.chips - 1 + self.grid.slot(i, j)
        return send(view, view, self.ssem.at[k], self.rsem.at[k], "dp", self.grid.mate)

    def start(self):
        for i in range(1, self.grid.first):
            self.chip(i, 0).start()
        for j in range(1, self.grid.second):
            self.chip(0, j).start()
        self.core(0, 0).start()

    def relay(self):
        for i in range(1, self.grid.first):
            self.chip(i, 0).wait_recv()
            for j in range(1, self.grid.second):
                self.chip(i, j).start()
            self.core(i, 0).start()

    def relay_rest(self):
        for i, j in self.grid.spots:
            if j > 0:
                self.chip(i, j).wait_recv()
                self.core(i, j).start()

    def last(self):
        for i, j in self.grid.spots:
            self.core(i, j).wait_recv()

    def finish(self):
        for i, j in self.grid.spots:
            if i > 0 or j > 0:
                self.chip(i, j).wait_send()
            self.core(i, j).wait_send()


class PlaneReduce:
    def __init__(self, parts, got, summed, land, grid, sems):
        self.parts, self.got, self.summed, self.land = parts, got, summed, land
        self.grid, self.sems = grid, sems

    def core(self):
        grid = self.grid
        part = self.parts.at[1 - grid.core_index]
        return send(part, self.got, self.sems[0], self.sems[1], "dp", grid.mate)

    def chip(self, i, j):
        k = self.grid.slot(i, j)
        target = self.grid.at(-i, 0) if j == 0 else self.grid.at(0, j)
        sems = self.sems[2].at[k - 1], self.sems[3].at[k - 1]
        return send(self.summed.at[k], self.land.at[k], *sems, "dp", target)

    def start(self):
        self.core().start()

    def pair(self, i, j):
        spot = lax.div(self.grid.at(-i, j), 2)
        return self.parts[self.grid.core_index, spot].astype(F32) + self.got[spot].astype(F32)

    def spread(self):
        self.core().wait_recv()
        for i, j in reversed(self.grid.spots):
            if j > 0:
                self.summed[self.grid.slot(i, j)] = self.pair(i, j).astype(BF)
                self.chip(i, j).start()

    def row(self, i):
        total = self.pair(i, 0)
        for j in range(1, self.grid.second):
            self.chip(i, j).wait_recv()
            total = total + self.land[self.grid.slot(i, j)].astype(F32)
        return total

    def spread_rest(self):
        for i in range(1, self.grid.first):
            self.summed[self.grid.slot(i, 0)] = self.row(i).astype(BF)
            self.chip(i, 0).start()

    def total(self):
        total = self.row(0)
        for i in range(1, self.grid.first):
            self.chip(i, 0).wait_recv()
            total = total + self.land[self.grid.slot(i, 0)].astype(F32)
        return total

    def finish(self):
        self.core().wait_send()
        for i, j in self.grid.spots:
            if i > 0 or j > 0:
                self.chip(i, j).wait_send()


def joined(value):
    parts, rows, columns = value.shape
    if rows % 16 == 0:
        return value.reshape(parts * rows, columns)
    return jnp.concatenate([value[d] for d in range(parts)], axis=0)


def put_parts(ref, value, *where):
    chips, rows = ref.shape[1], ref.shape[-2]
    for d in range(2 * chips):
        ref[(d % 2, d // 2) + where] = value[d * rows : (d + 1) * rows].astype(BF)


def layer_kernel(n, dp, names, *refs):
    r = SimpleNamespace(**dict(zip(names, refs)))
    me = lax.axis_index("tensor")
    mine = lax.axis_index("dp")
    chips = dp // 2
    chip = lax.div(mine, 2)
    core_mate = mine + 1 - 2 * lax.rem(mine, 2)
    pair_mate = me + 1 - 2 * lax.rem(me, 2)
    far = lax.rem(me + n // 2, n)
    own_rows, width = r.x.shape
    local = r.q.shape[1]
    units = r.ub.shape[-1]
    chunk = own_rows // CH
    scale = 1.0 / math.sqrt(HD)

    loads = {
        name: pltpu.make_async_copy(src, dst, r.lsem.at[k])
        for k, (name, src, dst) in enumerate(
            [
                ("x", r.x_h, r.x),
                ("qkv", r.qkv_h, r.aw.at[mine, pl.ds(0, 3)]),
                ("proj", r.proj_h, r.pv),
                ("down", r.down_h, r.ud.at[mine, 1]),
                ("up", r.up_h, r.ud.at[mine, 0]),
                ("ub", r.ub_h, r.ub.at[0]),
                ("qvb", r.qvb_h, r.qvb),
                ("bb", r.bb_h, r.bb),
                ("gain", r.gain_h, r.gain),
                ("nb", r.nb_h, r.nb),
                ("cot", r.cot_h, r.cot),
                ("lengths", r.lengths_h, r.lengths),
            ]
        )
    }
    for copy in loads.values():
        copy.start()
    barrier = pltpu.get_barrier_semaphore()
    for k in range(1, n):
        pl.semaphore_signal(
            barrier, inc=1, device_id={"tensor": lax.rem(me + k, n)}, device_id_type=MESH
        )
    for k in range(1, chips):
        pl.semaphore_signal(
            barrier, inc=1, device_id={"dp": lax.rem(mine + 2 * k, dp)}, device_id_type=MESH
        )
    pl.semaphore_signal(barrier, inc=1, device_id={"dp": core_mate}, device_id_type=MESH)

    loads["x"].wait()
    r.xr[me] = r.x[...].astype(BF)
    loads["proj"].wait()
    r.aw[mine, 3] = turned(r.pv[...])
    for name in ("qkv", "up", "down", "ub"):
        loads[name].wait()
    pl.semaphore_wait(barrier, n - 1 + chips)

    xg = ChainGather(r.xr, me, n, r.xg_s, r.xg_r)
    grids = [Plane(mine, dp, way) for way in range(3)]
    gathers = [
        PlaneGather(buf, grids[way], r.w_s.at[k], r.w_r.at[k])
        for k, (buf, way) in enumerate(((r.aw, 0), (r.ud, 1), (r.fu, 2), (r.fd, 2)))
    ]
    inner = jnp.logical_and(me > 0, me < n - 1)
    g_attn, g_ud, g_far_up, g_far_down = gathers

    def far_copy(k):
        src, dst = (
            (r.ud.at[mine, 0], r.fu.at[mine]),
            (r.ud.at[mine, 1], r.fd.at[mine]),
            (r.ub.at[0], r.ub.at[1]),
            (r.zs.at[0], r.zr.at[0]),
            (r.zs.at[1], r.zr.at[1]),
        )[k]
        return send(src, dst, r.z_s.at[k], r.z_r.at[k], "tensor", far)

    def pair_copy(phase, c, src, dst):
        return send(
            src.at[pl.ds(c * chunk, chunk)],
            dst.at[pl.ds(c * chunk, chunk)],
            r.p_s.at[phase % 2, c],
            r.p_r.at[phase % 2, c],
            "tensor",
            pair_mate,
        )

    def rows_of(c):
        return pl.ds(c * chunk, chunk)

    xg.steps(0)
    g_attn.start()
    g_ud.start()
    xg.steps(1)
    xg.steps(2)
    g_attn.relay()
    @pl.when(jnp.logical_not(inner))
    def _():
        for k in range(3):
            far_copy(k).start()

    for name in ("qvb", "bb", "gain", "nb", "cot", "lengths"):
        loads[name].wait()
    g_attn.last()
    xg.last()

    rounded = joined(r.xr[...])
    r.q[...] = (nn_dot(rounded, joined(r.aw[:, 0])) + r.qvb[0:1, :]).astype(BF)
    r.k[...] = nn_dot(rounded, joined(r.aw[:, 1])).astype(BF)
    r.v[...] = (nn_dot(rounded, joined(r.aw[:, 2])) + r.qvb[1:2, :]).astype(BF)
    @pl.when(inner)
    def _():
        for k in range(3):
            far_copy(k).start()

    seq_rows = r.q.shape[0]
    valid = lax.broadcasted_iota(jnp.int32, (seq_rows, seq_rows), 1) < r.lengths[0]
    heads = local // HD
    for head in range(heads):
        cols = slice(head * HD, (head + 1) * HD)
        scores = jnp.where(valid, nt_dot(r.q[:, cols], r.k[:, cols]) * scale, -1e30)
        weights = jnp.exp(scores - jnp.max(scores, axis=-1, keepdims=True))
        prob = weights * (1.0 / jnp.sum(weights, axis=-1, keepdims=True))
        r.prob[head] = prob
        r.ctx[:, cols] = nn_dot(prob.astype(BF), r.v[:, cols]).astype(BF)
    r.terms[...] = nt_dot(r.ctx[...], joined(r.aw[:, 3])).reshape(r.terms.shape)

    red = ChainReduce(r.terms, me, n, r.s1, r.r1, r.r1_s, r.r1_r)
    red.steps(0)
    g_ud.relay()
    far_copy(0).wait_recv()
    g_far_up.start()
    red.steps(1)
    far_copy(1).wait_recv()
    g_far_down.start()
    g_ud.relay_rest()
    red.steps(2)
    g_far_up.relay()
    g_far_down.relay()
    for c in range(CH):
        part = rows_of(c)
        red.total(c, r.acc)
        normed, inverse = layer_norm(r.x[part] + r.acc[part] + r.bb[0:1, :])
        middle = normed * r.gain[0:1, :] + r.nb[0:1, :]
        r.n1[part] = normed
        r.i1[part] = inverse
        r.mid[part] = middle
        r.m_all[0, part] = middle.astype(BF)
        pair_copy(0, c, r.m_all.at[0], r.m_all.at[1]).start()
    g_ud.last()
    g_far_up.relay_rest()
    far_copy(2).wait_recv()

    def up_of(h):
        return r.ud[:, 0] if h == 0 else r.fu[...]

    def down_of(h):
        return r.ud[:, 1] if h == 0 else r.fd[...]

    every = slice(0, own_rows)
    halves = [slice(c * chunk, (c + 1) * chunk) for c in range(CH)]

    def up_rows(group, h, part):
        cols = slice(h * units, (h + 1) * units)
        pre = nn_dot(r.m_all[group, part], joined(up_of(h))) + r.ub[h]
        r.pre[group, part, cols] = pre
        r.act[group, part, cols] = gelu_value(pre).astype(BF)

    def down_rows(group, part):
        return nt_dot(r.act[group, part, :units], joined(down_of(0))) + nt_dot(
            r.act[group, part, units:], joined(down_of(1))
        )

    up_rows(0, 0, every)
    g_far_up.last()
    up_rows(0, 1, every)
    g_far_down.relay_rest()
    for c, part in enumerate(halves):
        pair_copy(0, c, r.m_all.at[0], r.m_all.at[1]).wait_recv()
        up_rows(1, 0, part)
        up_rows(1, 1, part)
        if c == 0:
            g_far_down.last()
        r.ps[0, part] = down_rows(1, part).astype(BF)
        pair_copy(1, c, r.ps.at[0], r.pr.at[0]).start()
    r.acc[...] = down_rows(0, every)
    for group in range(2):
        for h in range(2):
            cols = slice(h * units, (h + 1) * units)
            r.pre[group, :, cols] = gelu_slope(r.pre[group, :, cols])

    for h in range(2):
        r.ut[h] = joined(up_of(h)).T
    for c in range(CH):
        part = rows_of(c)
        pair_copy(1, c, r.ps.at[0], r.pr.at[0]).wait_recv()
        normed, inverse = layer_norm(
            r.mid[part] + r.acc[part] + r.pr[0, part].astype(F32) + r.bb[1:2, :]
        )
        dres = norm_back(r.cot[part], normed, inverse, r.gain[1:2, :])
        r.d_all[0, part] = dres.astype(BF)
        pair_copy(0, c, r.m_all.at[0], r.m_all.at[1]).wait_send()
        pair_copy(2, c, r.d_all.at[0], r.d_all.at[1]).start()
        r.dres[part] = dres
        r.acc[part] = normed
    r.hidden_o[...] = r.acc[...] * r.gain[1:2, :] + r.nb[1:2, :]
    r.sums[3:4, :] = jnp.sum(r.cot[...] * r.acc[...], axis=0, keepdims=True)
    r.sums[4:5, :] = jnp.sum(r.cot[...], axis=0, keepdims=True)
    r.sums[5:6, :] = jnp.sum(r.dres[...], axis=0, keepdims=True)

    def back_rows(group, h, part):
        cols = slice(h * units, (h + 1) * units)
        dpre = nn_dot(r.d_all[group, part], joined(down_of(h))) * r.pre[group, part, cols]
        r.dpre[group, part, cols] = dpre.astype(BF)
        total = jnp.sum(dpre, axis=0, keepdims=True)
        r.sums[6 + h : 7 + h, :] = total if group == 0 else r.sums[6 + h : 7 + h, :] + total

    def up_back(group, part):
        return nn_dot(r.dpre[group, part, :units], r.ut[0]) + nn_dot(
            r.dpre[group, part, units:], r.ut[1]
        )

    back_rows(0, 0, every)
    back_rows(0, 1, every)
    for c, part in enumerate(halves):
        pair_copy(2, c, r.d_all.at[0], r.d_all.at[1]).wait_recv()
        back_rows(1, 0, part)
        back_rows(1, 1, part)
        r.ps[1, part] = up_back(1, part).astype(BF)
        pair_copy(1, c, r.ps.at[0], r.pr.at[0]).wait_send()
        pair_copy(3, c, r.ps.at[1], r.pr.at[1]).start()
    xg.finish()
    red.finish()
    reduces = {
        (h, t): PlaneReduce(
            r.g.at[h, t], r.gp.at[h, t], r.gs.at[h, t], r.gl.at[h, t], grids[0 if h else 1 + t],
            [sem.at[2 * h + t] for sem in (r.gc_s, r.gc_r, r.gx_s, r.gx_r)],
        )
        for h in range(2)
        for t in range(2)
    }

    def weight_part(h, t):
        cols = slice(h * units, (h + 1) * units)
        if t == 0:
            left, right = r.m_all[...], r.dpre[:, :, cols]
        else:
            left, right = r.d_all[...], r.act[:, :, cols]
        put_parts(r.g.at[h, t], tn_dot(joined(left), joined(right)))
        reduces[h, t].start()

    weight_part(1, 1)
    weight_part(1, 0)
    r.acc[...] = up_back(0, every) + r.dres[...]
    reduces[1, 1].spread()
    reduces[1, 1].spread_rest()
    weight_part(0, 1)
    weight_part(0, 0)
    dg = ChainGather(r.dr, me, n, r.xg_s, r.xg_r)
    for c in range(CH):
        part = rows_of(c)
        pair_copy(3, c, r.ps.at[1], r.pr.at[1]).wait_recv()
        dmid = r.acc[part] + r.pr[1, part].astype(F32)
        dres = norm_back(dmid, r.n1[part], r.i1[part], r.gain[0:1, :])
        r.dr[me, part] = dres.astype(BF)
        dg.step(0, c)
        r.acc[part] = dmid
        r.dres[part] = dres
    reduces[1, 0].spread()
    reduces[1, 0].spread_rest()
    r.sums[0:1, :] = jnp.sum(r.acc[...] * r.n1[...], axis=0, keepdims=True)
    r.sums[1:2, :] = jnp.sum(r.acc[...], axis=0, keepdims=True)
    r.sums[2:3, :] = jnp.sum(r.dres[...], axis=0, keepdims=True)

    def sum_mate():
        return send(r.sums, r.sp, r.m_s.at[0], r.m_r.at[0], "dp", core_mate)

    def bias_mate():
        return send(r.b, r.bp, r.m_s.at[1], r.m_r.at[1], "dp", core_mate)

    def bias_chip(k):
        view = r.bc.at[chip]
        sems = r.bc_s.at[k - 1], r.bc_r.at[k - 1]
        return send(view, view, *sems, "dp", lax.rem(mine + 2 * k, dp))

    def sum_chip(k):
        view = r.sc.at[chip]
        sems = r.sc_s.at[k - 1], r.sc_r.at[k - 1]
        return send(view, view, *sems, "dp", lax.rem(mine + 2 * k, dp))

    def sum_z(k):
        view = r.st.at[me]
        return send(view, view, r.st_s.at[k - 1], r.st_r.at[k - 1], "tensor", lax.rem(me + k, n))

    sum_mate().start()
    dg.steps(1)
    sum_mate().wait_recv()
    r.sc[chip] = r.sums[...] + r.sp[...]
    for k in range(1, chips):
        sum_chip(k).start()
    dg.steps(2)
    def far_total(t):
        r.zs[t] = reduces[1, t].total().astype(BF)

    far_total(1)

    @pl.when(jnp.logical_not(inner))
    def _():
        far_copy(4).start()
        far_total(0)
        far_copy(3).start()

    reduces[0, 1].spread()
    reduces[0, 0].spread()
    dg.last()

    for k in range(1, chips):
        sum_chip(k).wait_recv()
    total = r.sc[0]
    for k in range(1, chips):
        total = total + r.sc[k]
    r.st[me] = total
    for k in range(1, n):
        sum_z(k).start()
    @pl.when(inner)
    def _():
        far_copy(4).start()

    dres_all = joined(r.dr[...])
    r.dctx[...] = nn_dot(dres_all, joined(r.aw[:, 3])).astype(BF)
    r.b[...] = jnp.zeros_like(r.b)
    for head in range(heads):
        cols = slice(head * HD, (head + 1) * HD)
        prob = r.prob[head]
        dc = r.dctx[:, cols]
        dprob = nt_dot(dc, r.v[:, cols])
        weighted = jnp.sum(prob * dprob, axis=-1, keepdims=True)
        dscore = (prob * (dprob - weighted) * scale).astype(BF)
        dquery = nn_dot(dscore, r.k[:, cols])
        dvalue = tn_dot(prob.astype(BF), dc)
        r.dm[0, :, cols] = dquery.astype(BF)
        r.dm[1, :, cols] = tn_dot(dscore, r.q[:, cols]).astype(BF)
        r.dm[2, :, cols] = dvalue.astype(BF)
        r.b[0:1, cols] = jnp.sum(dquery, axis=0, keepdims=True)
        r.b[1:2, cols] = jnp.sum(dvalue, axis=0, keepdims=True)
    @pl.when(inner)
    def _():
        far_total(0)
        far_copy(3).start()

    bias_mate().start()
    dx = nt_dot(r.dm[0], joined(r.aw[:, 0]))
    for j in range(1, 3):
        dx = dx + nt_dot(r.dm[j], joined(r.aw[:, j]))
    r.terms[...] = dx.reshape(r.terms.shape)

    red_x = ChainReduce(r.terms, me, n, r.s2, r.r2, r.r1_s, r.r1_r)
    red_x.steps(0)
    bias_mate().wait_recv()
    r.bc[chip] = r.b[...] + r.bp[...]
    for k in range(1, chips):
        bias_chip(k).start()
    reduces[0, 1].spread_rest()
    reduces[0, 0].spread_rest()
    attn = PlaneReduce(
        r.a, r.ap, r.as_, r.al, grids[0], (r.ac_s, r.ac_r, r.ax_s, r.ax_r)
    )
    rounded = joined(r.xr[...])
    for j in range(3):
        put_parts(r.a, tn_dot(rounded, r.dm[j]), j)
    put_parts(r.a, tn_dot(joined(r.dr[...]), r.ctx[...]), 3)
    attn.start()
    red_x.steps(1)
    attn.spread()
    attn.spread_rest()
    red_x.steps(2)

    for k in range(1, n):
        sum_z(k).wait_recv()
    total = r.st[0]
    for k in range(1, n):
        total = total + r.st[k]
    for j in range(2):
        for k, ref in enumerate((r.gain_o, r.nb_o, r.branch_o)):
            ref[j : j + 1, :] = total[3 * j + k : 3 * j + k + 1]
    r.ub_o[...] = r.st[me, 6:7] + r.st[far, 7:8]
    for k in range(1, chips):
        bias_chip(k).wait_recv()
    total = r.bc[0]
    for k in range(1, chips):
        total = total + r.bc[k]
    r.qvb_o[...] = total[0:2]
    for c in range(CH):
        red_x.total(c, r.acc)
    r.dx_o[...] = r.acc[...] + r.dres[...]
    for t, out in enumerate((r.up_o, r.down_o)):
        out[...] = reduces[0, t].total()
    for t, out in ((1, r.down_o), (0, r.up_o)):
        far_copy(3 + t).wait_recv()
        out[...] += r.zr[t].astype(F32)
    total = attn.total()
    r.qkv_o[...] = total[0:3]
    r.proj_o[...] = total[3].T

    dg.finish()
    red_x.finish()
    for gather in gathers:
        gather.finish()
    for reduce in list(reduces.values()) + [attn]:
        reduce.finish()
    for k in range(5):
        far_copy(k).wait_send()
    for c in range(CH):
        pair_copy(2, c, r.d_all.at[0], r.d_all.at[1]).wait_send()
        pair_copy(3, c, r.ps.at[1], r.pr.at[1]).wait_send()
    sum_mate().wait_send()
    bias_mate().wait_send()
    for k in range(1, chips):
        sum_chip(k).wait_send()
        bias_chip(k).wait_send()
    for k in range(1, n):
        sum_z(k).wait_send()


def store_kernel(count, *refs):
    sems = refs[2 * count]
    copies = [
        pltpu.make_async_copy(refs[k], refs[count + k], sems.at[k]) for k in range(count)
    ]
    for copy in copies:
        copy.start()
    for copy in copies:
        copy.wait()


def per_device(
    inputs,
    lengths,
    qkv_weight,
    qv_bias,
    proj_weight,
    branch_bias,
    up_weight,
    up_bias,
    down_weight,
    norm_gain,
    norm_bias,
    cotangent,
):
    n = lax.axis_size("tensor")
    dp = lax.axis_size("dp")
    rows, width = inputs.shape
    shard, local = qkv_weight.shape[2:]
    units = up_weight.shape[2]
    chips = dp // 2
    seq = rows * n
    heads = local // HD
    dma = pltpu.SemaphoreType.DMA

    operands = {
        "lengths_h": lengths,
        "x_h": inputs,
        "qkv_h": qkv_weight[0],
        "qvb_h": qv_bias[0],
        "proj_h": proj_weight[0],
        "bb_h": branch_bias[0],
        "up_h": up_weight[0],
        "ub_h": up_bias,
        "down_h": down_weight[0].T,
        "gain_h": norm_gain[0],
        "nb_h": norm_bias[0],
        "cot_h": cotangent,
    }
    outs = {
        "hidden_o": (rows, width),
        "dx_o": (rows, width),
        "qkv_o": (3, shard, local),
        "qvb_o": (2, local),
        "proj_o": (local, shard),
        "branch_o": (2, width),
        "up_o": (shard, units),
        "ub_o": (1, units),
        "down_o": (shard, units),
        "gain_o": (2, width),
        "nb_o": (2, width),
    }
    chain = (2, n - 1, rows, width)
    buffers = {
        "x": ((rows, width), F32),
        "cot": ((rows, width), F32),
        "xr": ((n, rows, width), BF),
        "dr": ((n, rows, width), BF),
        "aw": ((dp, 4, shard, local), BF),
        "pv": ((local, shard), BF),
        "ud": ((dp, 2, shard, units), BF),
        "ut": ((2, units, width), BF),
        "fu": ((dp, shard, units), BF),
        "fd": ((dp, shard, units), BF),
        "qvb": ((2, local), F32),
        "bb": ((2, width), F32),
        "ub": ((2, 1, units), F32),
        "gain": ((2, width), F32),
        "nb": ((2, width), F32),
        "q": ((seq, local), BF),
        "k": ((seq, local), BF),
        "v": ((seq, local), BF),
        "ctx": ((seq, local), BF),
        "dctx": ((seq, local), BF),
        "dm": ((3, seq, local), BF),
        "prob": ((heads, seq, seq), F32),
        "terms": ((n, rows, width), F32),
        "s1": (chain, BF),
        "r1": (chain, BF),
        "s2": (chain, BF),
        "r2": (chain, BF),
        "acc": ((rows, width), F32),
        "n1": ((rows, width), F32),
        "i1": ((rows, 1), F32),
        "mid": ((rows, width), F32),
        "dres": ((rows, width), F32),
        "m_all": ((2, rows, width), BF),
        "d_all": ((2, rows, width), BF),
        "pre": ((2, rows, 2 * units), F32),
        "act": ((2, rows, 2 * units), BF),
        "dpre": ((2, rows, 2 * units), BF),
        "ps": ((2, rows, width), BF),
        "pr": ((2, rows, width), BF),
        "g": ((2, 2, 2, chips, shard, units), BF),
        "gp": ((2, 2, chips, shard, units), BF),
        "gs": ((2, 2, chips, shard, units), BF),
        "gl": ((2, 2, chips, shard, units), BF),
        "zs": ((2, shard, units), BF),
        "zr": ((2, shard, units), BF),
        "a": ((2, chips, 4, shard, local), BF),
        "ap": ((chips, 4, shard, local), BF),
        "as_": ((chips, 4, shard, local), BF),
        "al": ((chips, 4, shard, local), BF),
        "sums": ((8, width), F32),
        "sp": ((8, width), F32),
        "sc": ((chips, 8, width), F32),
        "st": ((n, 8, width), F32),
        "b": ((8, local), F32),
        "bp": ((8, local), F32),
        "bc": ((chips, 8, local), F32),
    }
    semaphores = {"lsem": (12,)}
    for name, shape in {
        "m": (2,),
        "z": (5,),
        "xg": (2, n - 1, CH),
        "r1": (2, n - 1, CH),
        "w": (4, 2 * chips - 1),
        "p": (2, CH),
        "gc": (4,),
        "gx": (4, chips - 1),
        "ac": (),
        "ax": (chips - 1,),
        "sc": (chips - 1,),
        "bc": (chips - 1,),
        "st": (n - 1,),
    }.items():
        semaphores[name + "_s"] = shape
        semaphores[name + "_r"] = shape
    names = list(operands) + list(outs) + list(buffers) + ["lengths"] + list(semaphores)

    vmem = pl.BlockSpec(memory_space=pltpu.VMEM)
    any_space = pl.BlockSpec(memory_space=pl.ANY)
    results = pl.pallas_call(
        functools.partial(layer_kernel, n, dp, names),
        out_shape=[pltpu.VMEM(shape, F32) for shape in outs.values()],
        in_specs=[any_space] * len(operands),
        out_specs=[vmem] * len(outs),
        scratch_shapes=[pltpu.VMEM(shape, kind) for shape, kind in buffers.values()]
        + [pltpu.SMEM(lengths.shape, jnp.int32)]
        + [dma(shape) if shape else dma for shape in semaphores.values()],
        compiler_params=pltpu.CompilerParams(
            collective_id=0, has_side_effects=True, vmem_limit_bytes=56 * 2**20
        ),
    )(*operands.values())
    shapes = [jax.ShapeDtypeStruct(shape, F32) for shape in outs.values()]
    hidden, dx, qkv, qvb, proj, branch, up, ub, down, gain, nb = pl.pallas_call(
        functools.partial(store_kernel, len(outs)),
        out_shape=shapes,
        in_specs=[vmem] * len(outs),
        out_specs=[any_space] * len(outs),
        scratch_shapes=[dma((len(outs),))],
    )(*[pltpu.with_memory_space_constraint(result, pltpu.VMEM) for result in results])
    return (
        hidden,
        dx,
        qkv[None],
        qvb[None],
        proj[None],
        branch[None],
        up[None],
        ub,
        down.T[None],
        gain[None],
        nb[None],
    )


def solution(mesh):
    placed = (
        P(("dp", "tensor"), None),
        P("dp"),
        P(None, None, "dp", "tensor"),
        P(None, None, "tensor"),
        P(None, "tensor", "dp"),
        P(),
        P(None, "dp", "tensor"),
        P(None, "tensor"),
        P(None, "tensor", "dp"),
        P(),
        P(),
        P(("dp", "tensor"), None),
    )
    return jax.shard_map(
        per_device,
        mesh=mesh,
        in_specs=placed,
        out_specs=(
            P(("dp", "tensor"), None),
            P(("dp", "tensor"), None),
            P(None, None, "dp", "tensor"),
            P(None, None, "tensor"),
            P(None, "tensor", "dp"),
            P(),
            P(None, "dp", "tensor"),
            P(None, "tensor"),
            P(None, "tensor", "dp"),
            P(),
            P(),
        ),
        check_vma=False,
    )
```

```python
import functools
import math
from types import SimpleNamespace

import jax
import jax.numpy as jnp
from jax import lax
from jax.experimental import pallas as pl
from jax.experimental.pallas import tpu as pltpu
from jax.sharding import PartitionSpec as P

MESH = pl.DeviceIdType.MESH
BF = jnp.bfloat16
F32 = jnp.float32
HD = 64
CH = 2

norm_eps = 1e-12
half_root = 0.7071067811865476
inv_root = 0.3989422804014327


def layer_norm(residual):
    centred = residual - jnp.mean(residual, axis=-1, keepdims=True)
    inverse = lax.rsqrt(jnp.mean(centred * centred, axis=-1, keepdims=True) + norm_eps)
    return (centred * inverse, inverse)


def norm_back(upstream, normed, inverse, gain_row):
    scaled = upstream * gain_row
    return inverse * (
        scaled
        - jnp.mean(scaled, axis=-1, keepdims=True)
        - normed * jnp.mean(scaled * normed, axis=-1, keepdims=True)
    )


def gelu_value(pre_act):
    return 0.5 * pre_act * (1.0 + lax.erf(pre_act * half_root))


def gelu_slope(pre_act):
    return (
        0.5 * (1.0 + lax.erf(pre_act * half_root))
        + pre_act * jnp.exp(-0.5 * pre_act * pre_act) * inv_root
    )


def nn_dot(left, right):
    return jnp.dot(left, right, preferred_element_type=F32)


def nt_dot(left, right):
    return lax.dot_general(left, right, (((1,), (1,)), ((), ())), preferred_element_type=F32)


def tn_dot(left, right):
    return lax.dot_general(left, right, (((0,), (0,)), ((), ())), preferred_element_type=F32)


def turned(block):
    size = block.shape[1]
    row = lax.broadcasted_iota(jnp.int32, (size, size), 0)
    col = lax.broadcasted_iota(jnp.int32, (size, size), 1)
    return nt_dot(jnp.where(row == col, 1.0, 0.0).astype(BF), block).astype(BF)


def send(src, dst, send_sem, recv_sem, axis, target):
    return pltpu.make_async_remote_copy(
        src_ref=src,
        dst_ref=dst,
        send_sem=send_sem,
        recv_sem=recv_sem,
        device_id={axis: target},
        device_id_type=MESH,
    )


def ways(me, n):
    return ((0, me, me + 1), (1, n - 1 - me, me - 1))


class ChainGather:
    def __init__(self, buf, me, n, ssem, rsem):
        self.buf, self.me, self.n, self.ssem, self.rsem = buf, me, n, ssem, rsem
        self.chunk = buf.shape[1] // CH

    def link(self, way, s, c, pos, target):
        block = pos - s
        block = block if way == 0 else self.n - 1 - block
        view = self.buf.at[block, pl.ds(c * self.chunk, self.chunk)]
        sems = self.ssem.at[way, s, c], self.rsem.at[way, s, c]
        return send(view, view, *sems, "tensor", target)

    def step(self, s, c):
        for way, pos, target in ways(self.me, self.n):

            @pl.when(jnp.logical_and(pos >= s, pos < self.n - 1))
            def _(way=way, pos=pos, target=target):
                if s > 0:
                    self.link(way, s - 1, c, pos - 1, target).wait_recv()
                self.link(way, s, c, pos, target).start()

    def steps(self, s):
        for c in range(CH):
            self.step(s, c)

    def last(self):
        for way, pos, target in ways(self.me, self.n):

            @pl.when(pos == self.n - 1)
            def _(way=way, pos=pos, target=target):
                for s in range(self.n - 1):
                    for c in range(CH):
                        self.link(way, s, c, pos - 1, target).wait_recv()

    def finish(self):
        for s in range(self.n - 1):
            for way, pos, target in ways(self.me, self.n):

                @pl.when(jnp.logical_and(pos >= s, pos < self.n - 1))
                def _(way=way, pos=pos, target=target):
                    for c in range(CH):
                        self.link(way, s, c, pos, target).wait_send()


class ChainReduce:
    def __init__(self, terms, me, n, sbuf, rbuf, ssem, rsem):
        self.terms, self.me, self.n = terms, me, n
        self.sbuf, self.rbuf, self.ssem, self.rsem = sbuf, rbuf, ssem, rsem
        self.chunk = terms.shape[1] // CH

    def part(self, c):
        return pl.ds(c * self.chunk, self.chunk)

    def link(self, way, s, c, target):
        return send(
            self.sbuf.at[way, s, self.part(c)],
            self.rbuf.at[way, s, self.part(c)],
            self.ssem.at[way, s, c],
            self.rsem.at[way, s, c],
            "tensor",
            target,
        )

    def step(self, s, c):
        for way, pos, target in ways(self.me, self.n):
            owner = self.n - 1 - s + pos
            block = owner if way == 0 else self.n - 1 - owner

            @pl.when(pos <= s)
            def _(way=way, pos=pos, target=target, block=block):
                if s == 0:
                    self.sbuf[way, s, self.part(c)] = self.terms[block, self.part(c)].astype(BF)
                else:

                    @pl.when(pos == 0)
                    def _():
                        self.link(way, s - 1, c, target).wait_send()
                        self.sbuf[way, s, self.part(c)] = self.terms[block, self.part(c)].astype(BF)

                    @pl.when(pos > 0)
                    def _():
                        self.link(way, s - 1, c, target).wait_recv()
                        got = self.rbuf[way, s - 1, self.part(c)].astype(F32)
                        self.sbuf[way, s, self.part(c)] = (
                            self.terms[block, self.part(c)] + got
                        ).astype(BF)

                self.link(way, s, c, target).start()

    def steps(self, s):
        for c in range(CH):
            self.step(s, c)

    def total(self, c, acc):
        acc[self.part(c)] = self.terms[self.me, self.part(c)]
        for way, pos, target in ways(self.me, self.n):

            @pl.when(pos > 0)
            def _(way=way, target=target):
                self.link(way, self.n - 2, c, target).wait_recv()
                acc[self.part(c)] += self.rbuf[way, self.n - 2, self.part(c)].astype(F32)

    def finish(self):
        for s in range(self.n - 1):
            for way, pos, target in ways(self.me, self.n):

                @pl.when(jnp.logical_and(pos <= s, jnp.logical_or(pos > 0, s == self.n - 2)))
                def _(way=way, target=target):
                    for c in range(CH):
                        self.link(way, s, c, target).wait_send()


class Plane:
    def __init__(self, mine, dp, way):
        chips = dp // 2
        chip = lax.div(mine, 2)
        self.core_index = lax.rem(mine, 2)
        self.mate = mine + 1 - 2 * self.core_index
        self.way = way
        if way == 0:
            self.first, self.second = chips, 1
            self.f, self.g = chip, 0
        elif way == 1:
            self.first, self.second = 2, chips // 2
            self.f, self.g = lax.rem(chip, 2), lax.div(chip, 2)
        else:
            self.first, self.second = chips // 2, 2
            self.f, self.g = lax.div(chip, 2), lax.rem(chip, 2)
        self.spots = [(i, j) for j in range(self.second) for i in range(self.first)]

    def at(self, i, j, other_core=False):
        f = lax.rem(self.f + i % self.first, self.first)
        g = lax.rem(self.g + j % self.second, self.second) if self.second > 1 else 0
        chip = f if self.way == 0 else (2 * g + f if self.way == 1 else 2 * f + g)
        return 2 * chip + (1 - self.core_index if other_core else self.core_index)

    def slot(self, i, j):
        return i * self.second + j


class PlaneGather:
    def __init__(self, buf, grid, ssem, rsem):
        self.buf, self.grid, self.ssem, self.rsem = buf, grid, ssem, rsem
        self.chips = grid.first * grid.second

    def chip(self, i, j):
        k = self.grid.slot(i, j) - 1
        sems = self.ssem.at[k], self.rsem.at[k]
        if j == 0:
            view, target = self.buf.at[self.grid.at(0, 0)], self.grid.at(i, 0)
        else:
            view, target = self.buf.at[self.grid.at(-i, 0)], self.grid.at(0, j)
        return send(view, view, *sems, "dp", target)

    def core(self, i, j):
        view = self.buf.at[self.grid.at(-i, -j)]
        k = self.chips - 1 + self.grid.slot(i, j)
        return send(view, view, self.ssem.at[k], self.rsem.at[k], "dp", self.grid.mate)

    def start(self):
        for i in range(1, self.grid.first):
            self.chip(i, 0).start()
        for j in range(1, self.grid.second):
            self.chip(0, j).start()
        self.core(0, 0).start()

    def relay(self):
        for i in range(1, self.grid.first):
            self.chip(i, 0).wait_recv()
            for j in range(1, self.grid.second):
                self.chip(i, j).start()
            self.core(i, 0).start()

    def relay_rest(self):
        for i, j in self.grid.spots:
            if j > 0:
                self.chip(i, j).wait_recv()
                self.core(i, j).start()

    def last(self):
        for i, j in self.grid.spots:
            self.core(i, j).wait_recv()

    def finish(self):
        for i, j in self.grid.spots:
            if i > 0 or j > 0:
                self.chip(i, j).wait_send()
            self.core(i, j).wait_send()


class PlaneReduce:
    def __init__(self, parts, got, summed, land, grid, sems):
        self.parts, self.got, self.summed, self.land = parts, got, summed, land
        self.grid, self.sems = grid, sems

    def core(self):
        grid = self.grid
        part = self.parts.at[1 - grid.core_index]
        return send(part, self.got, self.sems[0], self.sems[1], "dp", grid.mate)

    def chip(self, i, j):
        k = self.grid.slot(i, j)
        target = self.grid.at(-i, 0) if j == 0 else self.grid.at(0, j)
        sems = self.sems[2].at[k - 1], self.sems[3].at[k - 1]
        return send(self.summed.at[k], self.land.at[k], *sems, "dp", target)

    def start(self):
        self.core().start()

    def pair(self, i, j):
        spot = lax.div(self.grid.at(-i, j), 2)
        return self.parts[self.grid.core_index, spot].astype(F32) + self.got[spot].astype(F32)

    def spread(self):
        self.core().wait_recv()
        for i, j in reversed(self.grid.spots):
            if j > 0:
                self.summed[self.grid.slot(i, j)] = self.pair(i, j).astype(BF)
                self.chip(i, j).start()

    def row(self, i):
        total = self.pair(i, 0)
        for j in range(1, self.grid.second):
            self.chip(i, j).wait_recv()
            total = total + self.land[self.grid.slot(i, j)].astype(F32)
        return total

    def spread_rest(self):
        for i in range(1, self.grid.first):
            self.summed[self.grid.slot(i, 0)] = self.row(i).astype(BF)
            self.chip(i, 0).start()

    def total(self):
        total = self.row(0)
        for i in range(1, self.grid.first):
            self.chip(i, 0).wait_recv()
            total = total + self.land[self.grid.slot(i, 0)].astype(F32)
        return total

    def finish(self):
        self.core().wait_send()
        for i, j in self.grid.spots:
            if i > 0 or j > 0:
                self.chip(i, j).wait_send()


def joined(value):
    parts, rows, columns = value.shape
    if rows % 16 == 0:
        return value.reshape(parts * rows, columns)
    return jnp.concatenate([value[d] for d in range(parts)], axis=0)


def put_parts(ref, value, *where):
    chips, rows = ref.shape[1], ref.shape[-2]
    for d in range(2 * chips):
        ref[(d % 2, d // 2) + where] = value[d * rows : (d + 1) * rows].astype(BF)


def layer_kernel(n, dp, names, *refs):
    r = SimpleNamespace(**dict(zip(names, refs)))
    me = lax.axis_index("tensor")
    mine = lax.axis_index("dp")
    chips = dp // 2
    chip = lax.div(mine, 2)
    core_mate = mine + 1 - 2 * lax.rem(mine, 2)
    pair_mate = me + 1 - 2 * lax.rem(me, 2)
    far = lax.rem(me + n // 2, n)
    own_rows, width = r.x.shape
    local = r.q.shape[1]
    units = r.ub.shape[-1]
    chunk = own_rows // CH
    scale = 1.0 / math.sqrt(HD)

    loads = {
        name: pltpu.make_async_copy(src, dst, r.lsem.at[k])
        for k, (name, src, dst) in enumerate(
            [
                ("x", r.x_h, r.x),
                ("qkv", r.qkv_h, r.aw.at[mine, pl.ds(0, 3)]),
                ("proj", r.proj_h, r.pv),
                ("down", r.down_h, r.nd.at[mine]),
                ("up", r.up_h, r.nu.at[mine]),
                ("ub", r.ub_h, r.ub.at[0]),
                ("qvb", r.qvb_h, r.qvb),
                ("bb", r.bb_h, r.bb),
                ("gain", r.gain_h, r.gain),
                ("nb", r.nb_h, r.nb),
                ("cot", r.cot_h, r.cot),
                ("lengths", r.lengths_h, r.lengths),
            ]
        )
    }
    for copy in loads.values():
        copy.start()
    barrier = pltpu.get_barrier_semaphore()
    for k in range(1, n):
        pl.semaphore_signal(
            barrier, inc=1, device_id={"tensor": lax.rem(me + k, n)}, device_id_type=MESH
        )
    for k in range(1, chips):
        pl.semaphore_signal(
            barrier, inc=1, device_id={"dp": lax.rem(mine + 2 * k, dp)}, device_id_type=MESH
        )
    pl.semaphore_signal(barrier, inc=1, device_id={"dp": core_mate}, device_id_type=MESH)

    loads["x"].wait()
    r.xr[me] = r.x[...].astype(BF)
    loads["proj"].wait()
    r.aw[mine, 3] = turned(r.pv[...])
    for name in ("qkv", "up", "down", "ub"):
        loads[name].wait()
    pl.semaphore_wait(barrier, n - 1 + chips)

    xg = ChainGather(r.xr, me, n, r.xg_s, r.xg_r)
    grids = [Plane(mine, dp, way) for way in range(3)]
    gathers = [
        PlaneGather(buf, grids[way], r.w_s.at[k], r.w_r.at[k])
        for k, (buf, way) in enumerate(((r.aw, 0), (r.nu, 1), (r.nd, 2), (r.fu, 1), (r.fd, 2)))
    ]
    inner = jnp.logical_and(me > 0, me < n - 1)
    g_attn, g_up, g_down, g_far_up, g_far_down = gathers

    def far_copy(k):
        src, dst = (
            (r.nu.at[mine], r.fu.at[mine]),
            (r.nd.at[mine], r.fd.at[mine]),
            (r.ub.at[0], r.ub.at[1]),
            (r.zs.at[0], r.zr.at[0]),
            (r.zs.at[1], r.zr.at[1]),
        )[k]
        return send(src, dst, r.z_s.at[k], r.z_r.at[k], "tensor", far)

    def pair_copy(phase, c, src, dst):
        return send(
            src.at[pl.ds(c * chunk, chunk)],
            dst.at[pl.ds(c * chunk, chunk)],
            r.p_s.at[phase % 2, c],
            r.p_r.at[phase % 2, c],
            "tensor",
            pair_mate,
        )

    def rows_of(c):
        return pl.ds(c * chunk, chunk)

    xg.steps(0)
    g_attn.start()
    g_up.start()
    g_down.start()
    xg.steps(1)
    xg.steps(2)
    g_attn.relay()
    @pl.when(jnp.logical_not(inner))
    def _():
        for k in range(3):
            far_copy(k).start()

    for name in ("qvb", "bb", "gain", "nb", "cot", "lengths"):
        loads[name].wait()
    g_attn.last()
    xg.last()

    rounded = joined(r.xr[...])
    r.q[...] = (nn_dot(rounded, joined(r.aw[:, 0])) + r.qvb[0:1, :]).astype(BF)
    r.k[...] = nn_dot(rounded, joined(r.aw[:, 1])).astype(BF)
    r.v[...] = (nn_dot(rounded, joined(r.aw[:, 2])) + r.qvb[1:2, :]).astype(BF)
    @pl.when(inner)
    def _():
        for k in range(3):
            far_copy(k).start()

    g_up.relay()
    g_down.relay()
    seq_rows = r.q.shape[0]
    valid = lax.broadcasted_iota(jnp.int32, (seq_rows, seq_rows), 1) < r.lengths[0]
    heads = local // HD
    for head in range(heads):
        cols = slice(head * HD, (head + 1) * HD)
        scores = jnp.where(valid, nt_dot(r.q[:, cols], r.k[:, cols]) * scale, -1e30)
        weights = jnp.exp(scores - jnp.max(scores, axis=-1, keepdims=True))
        prob = weights * (1.0 / jnp.sum(weights, axis=-1, keepdims=True))
        r.prob[head] = prob
        r.ctx[:, cols] = nn_dot(prob.astype(BF), r.v[:, cols]).astype(BF)
    r.terms[...] = nt_dot(r.ctx[...], joined(r.aw[:, 3])).reshape(r.terms.shape)

    red = ChainReduce(r.terms, me, n, r.s1, r.r1, r.r1_s, r.r1_r)
    red.steps(0)
    far_copy(0).wait_recv()
    g_far_up.start()
    red.steps(1)
    far_copy(1).wait_recv()
    g_far_down.start()
    g_up.relay_rest()
    g_down.relay_rest()
    red.steps(2)
    g_far_up.relay()
    g_far_down.relay()
    g_up.last()
    g_down.last()
    r.dt[...] = joined(r.nd[...]).T
    r.ut[0] = joined(r.nu[...]).T
    for c in range(CH):
        part = rows_of(c)
        red.total(c, r.acc)
        normed, inverse = layer_norm(r.x[part] + r.acc[part] + r.bb[0:1, :])
        middle = normed * r.gain[0:1, :] + r.nb[0:1, :]
        r.n1[part] = normed
        r.i1[part] = inverse
        r.mid[part] = middle
        r.m_all[0, part] = middle.astype(BF)
        pair_copy(0, c, r.m_all.at[0], r.m_all.at[1]).start()
    g_far_up.relay_rest()
    far_copy(2).wait_recv()

    def up_of(h):
        return r.nu[...] if h == 0 else r.fu[...]

    def down_of(h):
        return r.nd[...] if h == 0 else r.fd[...]

    every = slice(0, own_rows)
    halves = [slice(c * chunk, (c + 1) * chunk) for c in range(CH)]

    def up_rows(group, h, part):
        cols = slice(h * units, (h + 1) * units)
        pre = nn_dot(r.m_all[group, part], joined(up_of(h))) + r.ub[h]
        r.pre[group, part, cols] = pre
        r.act[group, part, cols] = gelu_value(pre).astype(BF)

    def down_rows(group, part):
        return nn_dot(r.act[group, part, :units], r.dt[...]) + nt_dot(
            r.act[group, part, units:], joined(down_of(1))
        )

    up_rows(0, 0, every)
    for c, part in enumerate(halves):
        pair_copy(0, c, r.m_all.at[0], r.m_all.at[1]).wait_recv()
        up_rows(1, 0, part)
        if c == 0:
            g_far_up.last()
        up_rows(1, 1, part)
        if c == 0:
            g_far_down.relay_rest()
            g_far_down.last()
        r.ps[0, part] = down_rows(1, part).astype(BF)
        pair_copy(1, c, r.ps.at[0], r.pr.at[0]).start()
    up_rows(0, 1, every)
    r.acc[...] = down_rows(0, every)
    for group in range(2):
        for h in range(2):
            cols = slice(h * units, (h + 1) * units)
            r.pre[group, :, cols] = gelu_slope(r.pre[group, :, cols])

    r.ut[1] = joined(up_of(1)).T
    for c in range(CH):
        part = rows_of(c)
        pair_copy(1, c, r.ps.at[0], r.pr.at[0]).wait_recv()
        normed, inverse = layer_norm(
            r.mid[part] + r.acc[part] + r.pr[0, part].astype(F32) + r.bb[1:2, :]
        )
        dres = norm_back(r.cot[part], normed, inverse, r.gain[1:2, :])
        r.d_all[0, part] = dres.astype(BF)
        pair_copy(0, c, r.m_all.at[0], r.m_all.at[1]).wait_send()
        pair_copy(2, c, r.d_all.at[0], r.d_all.at[1]).start()
        r.dres[part] = dres
        r.acc[part] = normed
    r.hidden_o[...] = r.acc[...] * r.gain[1:2, :] + r.nb[1:2, :]
    r.sums[3:4, :] = jnp.sum(r.cot[...] * r.acc[...], axis=0, keepdims=True)
    r.sums[4:5, :] = jnp.sum(r.cot[...], axis=0, keepdims=True)
    r.sums[5:6, :] = jnp.sum(r.dres[...], axis=0, keepdims=True)

    def back_rows(group, h, part):
        cols = slice(h * units, (h + 1) * units)
        dpre = nn_dot(r.d_all[group, part], joined(down_of(h))) * r.pre[group, part, cols]
        r.dpre[group, part, cols] = dpre.astype(BF)
        total = jnp.sum(dpre, axis=0, keepdims=True)
        r.sums[6 + h : 7 + h, :] = total if group == 0 else r.sums[6 + h : 7 + h, :] + total

    def up_back(group, part):
        return nn_dot(r.dpre[group, part, :units], r.ut[0]) + nn_dot(
            r.dpre[group, part, units:], r.ut[1]
        )

    back_rows(0, 0, every)
    back_rows(0, 1, every)
    for c, part in enumerate(halves):
        pair_copy(2, c, r.d_all.at[0], r.d_all.at[1]).wait_recv()
        back_rows(1, 0, part)
        back_rows(1, 1, part)
        r.ps[1, part] = up_back(1, part).astype(BF)
        pair_copy(1, c, r.ps.at[0], r.pr.at[0]).wait_send()
        pair_copy(3, c, r.ps.at[1], r.pr.at[1]).start()
    xg.finish()
    red.finish()
    reduces = {
        (h, t): PlaneReduce(
            r.g.at[h, t], r.gp.at[h, t], r.gs.at[h, t], r.gl.at[h, t], grids[0 if h else 1 + t],
            [sem.at[2 * h + t] for sem in (r.gc_s, r.gc_r, r.gx_s, r.gx_r)],
        )
        for h in range(2)
        for t in range(2)
    }

    def weight_part(h, t):
        cols = slice(h * units, (h + 1) * units)
        if t == 0:
            left, right = r.m_all[...], r.dpre[:, :, cols]
        else:
            left, right = r.d_all[...], r.act[:, :, cols]
        put_parts(r.g.at[h, t], tn_dot(joined(left), joined(right)))
        reduces[h, t].start()

    weight_part(1, 1)
    weight_part(1, 0)
    r.acc[...] = up_back(0, every) + r.dres[...]
    reduces[1, 1].spread()
    reduces[1, 1].spread_rest()
    weight_part(0, 1)
    weight_part(0, 0)
    dg = ChainGather(r.dr, me, n, r.xg_s, r.xg_r)
    for c in range(CH):
        part = rows_of(c)
        pair_copy(3, c, r.ps.at[1], r.pr.at[1]).wait_recv()
        dmid = r.acc[part] + r.pr[1, part].astype(F32)
        dres = norm_back(dmid, r.n1[part], r.i1[part], r.gain[0:1, :])
        r.dr[me, part] = dres.astype(BF)
        dg.step(0, c)
        r.acc[part] = dmid
        r.dres[part] = dres
    reduces[1, 0].spread()
    reduces[1, 0].spread_rest()
    r.sums[0:1, :] = jnp.sum(r.acc[...] * r.n1[...], axis=0, keepdims=True)
    r.sums[1:2, :] = jnp.sum(r.acc[...], axis=0, keepdims=True)
    r.sums[2:3, :] = jnp.sum(r.dres[...], axis=0, keepdims=True)

    def sum_mate():
        return send(r.sums, r.sp, r.m_s.at[0], r.m_r.at[0], "dp", core_mate)

    def bias_mate():
        return send(r.b, r.bp, r.m_s.at[1], r.m_r.at[1], "dp", core_mate)

    def bias_chip(k):
        view = r.bc.at[chip]
        sems = r.bc_s.at[k - 1], r.bc_r.at[k - 1]
        return send(view, view, *sems, "dp", lax.rem(mine + 2 * k, dp))

    def sum_chip(k):
        view = r.sc.at[chip]
        sems = r.sc_s.at[k - 1], r.sc_r.at[k - 1]
        return send(view, view, *sems, "dp", lax.rem(mine + 2 * k, dp))

    def sum_pair():
        return send(r.st.at[0], r.st.at[1], r.st_s.at[0], r.st_r.at[0], "tensor", pair_mate)

    def sum_far():
        return send(r.st.at[2], r.st.at[3], r.st_s.at[1], r.st_r.at[1], "tensor", far)

    sum_mate().start()
    dg.steps(1)
    sum_mate().wait_recv()
    r.sc[chip] = r.sums[...] + r.sp[...]
    for k in range(1, chips):
        sum_chip(k).start()
    dg.steps(2)
    def far_total(t):
        r.zs[t] = reduces[1, t].total().astype(BF)

    far_total(1)

    @pl.when(jnp.logical_not(inner))
    def _():
        far_copy(4).start()
        far_total(0)
        far_copy(3).start()

    reduces[0, 1].spread()
    reduces[0, 0].spread()
    dg.last()

    for k in range(1, chips):
        sum_chip(k).wait_recv()
    total = r.sc[0]
    for k in range(1, chips):
        total = total + r.sc[k]
    r.st[0] = total
    sum_pair().start()
    @pl.when(inner)
    def _():
        far_copy(4).start()

    dres_all = joined(r.dr[...])
    r.dctx[...] = nn_dot(dres_all, joined(r.aw[:, 3])).astype(BF)
    r.b[...] = jnp.zeros_like(r.b)
    for head in range(heads):
        cols = slice(head * HD, (head + 1) * HD)
        prob = r.prob[head]
        dc = r.dctx[:, cols]
        dprob = nt_dot(dc, r.v[:, cols])
        weighted = jnp.sum(prob * dprob, axis=-1, keepdims=True)
        dscore = (prob * (dprob - weighted) * scale).astype(BF)
        dquery = nn_dot(dscore, r.k[:, cols])
        dvalue = tn_dot(prob.astype(BF), dc)
        r.dm[0, :, cols] = dquery.astype(BF)
        r.dm[1, :, cols] = tn_dot(dscore, r.q[:, cols]).astype(BF)
        r.dm[2, :, cols] = dvalue.astype(BF)
        r.b[0:1, cols] = jnp.sum(dquery, axis=0, keepdims=True)
        r.b[1:2, cols] = jnp.sum(dvalue, axis=0, keepdims=True)
    @pl.when(inner)
    def _():
        far_total(0)
        far_copy(3).start()

    bias_mate().start()
    sum_pair().wait_recv()
    r.st[2, 0:6] = r.st[0, 0:6] + r.st[1, 0:6]
    r.st[2, 6:8] = r.st[0, 6:8]
    sum_far().start()
    dx = nt_dot(r.dm[0], joined(r.aw[:, 0]))
    for j in range(1, 3):
        dx = dx + nt_dot(r.dm[j], joined(r.aw[:, j]))
    r.terms[...] = dx.reshape(r.terms.shape)

    red_x = ChainReduce(r.terms, me, n, r.s2, r.r2, r.r1_s, r.r1_r)
    red_x.steps(0)
    bias_mate().wait_recv()
    r.bc[chip] = r.b[...] + r.bp[...]
    for k in range(1, chips):
        bias_chip(k).start()
    reduces[0, 1].spread_rest()
    reduces[0, 0].spread_rest()
    attn = PlaneReduce(
        r.a, r.ap, r.as_, r.al, grids[0], (r.ac_s, r.ac_r, r.ax_s, r.ax_r)
    )
    rounded = joined(r.xr[...])
    for j in range(3):
        put_parts(r.a, tn_dot(rounded, r.dm[j]), j)
    put_parts(r.a, tn_dot(joined(r.dr[...]), r.ctx[...]), 3)
    attn.start()
    red_x.steps(1)
    attn.spread()
    attn.spread_rest()
    red_x.steps(2)

    sum_far().wait_recv()
    total = r.st[2] + r.st[3]
    for j in range(2):
        for k, ref in enumerate((r.gain_o, r.nb_o, r.branch_o)):
            ref[j : j + 1, :] = total[3 * j + k : 3 * j + k + 1]
    r.ub_o[...] = r.st[0, 6:7] + r.st[3, 7:8]
    for k in range(1, chips):
        bias_chip(k).wait_recv()
    total = r.bc[0]
    for k in range(1, chips):
        total = total + r.bc[k]
    r.qvb_o[...] = total[0:2]
    for c in range(CH):
        red_x.total(c, r.acc)
    r.dx_o[...] = r.acc[...] + r.dres[...]
    for t, out in enumerate((r.up_o, r.down_o)):
        out[...] = reduces[0, t].total()
    for t, out in ((1, r.down_o), (0, r.up_o)):
        far_copy(3 + t).wait_recv()
        out[...] += r.zr[t].astype(F32)
    total = attn.total()
    r.qkv_o[...] = total[0:3]
    r.proj_o[...] = total[3].T

    dg.finish()
    red_x.finish()
    for gather in gathers:
        gather.finish()
    for reduce in list(reduces.values()) + [attn]:
        reduce.finish()
    for k in range(5):
        far_copy(k).wait_send()
    for c in range(CH):
        pair_copy(2, c, r.d_all.at[0], r.d_all.at[1]).wait_send()
        pair_copy(3, c, r.ps.at[1], r.pr.at[1]).wait_send()
    sum_mate().wait_send()
    bias_mate().wait_send()
    for k in range(1, chips):
        sum_chip(k).wait_send()
        bias_chip(k).wait_send()
    sum_pair().wait_send()
    sum_far().wait_send()


def store_kernel(count, *refs):
    sems = refs[2 * count]
    copies = [
        pltpu.make_async_copy(refs[k], refs[count + k], sems.at[k]) for k in range(count)
    ]
    for copy in copies:
        copy.start()
    for copy in copies:
        copy.wait()


def per_device(
    inputs,
    lengths,
    qkv_weight,
    qv_bias,
    proj_weight,
    branch_bias,
    up_weight,
    up_bias,
    down_weight,
    norm_gain,
    norm_bias,
    cotangent,
):
    n = lax.axis_size("tensor")
    dp = lax.axis_size("dp")
    rows, width = inputs.shape
    shard, local = qkv_weight.shape[2:]
    units = up_weight.shape[2]
    chips = dp // 2
    seq = rows * n
    heads = local // HD
    dma = pltpu.SemaphoreType.DMA

    operands = {
        "lengths_h": lengths,
        "x_h": inputs,
        "qkv_h": qkv_weight[0],
        "qvb_h": qv_bias[0],
        "proj_h": proj_weight[0],
        "bb_h": branch_bias[0],
        "up_h": up_weight[0],
        "ub_h": up_bias,
        "down_h": down_weight[0].T,
        "gain_h": norm_gain[0],
        "nb_h": norm_bias[0],
        "cot_h": cotangent,
    }
    outs = {
        "hidden_o": (rows, width),
        "dx_o": (rows, width),
        "qkv_o": (3, shard, local),
        "qvb_o": (2, local),
        "proj_o": (local, shard),
        "branch_o": (2, width),
        "up_o": (shard, units),
        "ub_o": (1, units),
        "down_o": (shard, units),
        "gain_o": (2, width),
        "nb_o": (2, width),
    }
    chain = (2, n - 1, rows, width)
    buffers = {
        "x": ((rows, width), F32),
        "cot": ((rows, width), F32),
        "xr": ((n, rows, width), BF),
        "dr": ((n, rows, width), BF),
        "aw": ((dp, 4, shard, local), BF),
        "pv": ((local, shard), BF),
        "nu": ((dp, shard, units), BF),
        "nd": ((dp, shard, units), BF),
        "dt": ((units, width), BF),
        "ut": ((2, units, width), BF),
        "fu": ((dp, shard, units), BF),
        "fd": ((dp, shard, units), BF),
        "qvb": ((2, local), F32),
        "bb": ((2, width), F32),
        "ub": ((2, 1, units), F32),
        "gain": ((2, width), F32),
        "nb": ((2, width), F32),
        "q": ((seq, local), BF),
        "k": ((seq, local), BF),
        "v": ((seq, local), BF),
        "ctx": ((seq, local), BF),
        "dctx": ((seq, local), BF),
        "dm": ((3, seq, local), BF),
        "prob": ((heads, seq, seq), F32),
        "terms": ((n, rows, width), F32),
        "s1": (chain, BF),
        "r1": (chain, BF),
        "s2": (chain, BF),
        "r2": (chain, BF),
        "acc": ((rows, width), F32),
        "n1": ((rows, width), F32),
        "i1": ((rows, 1), F32),
        "mid": ((rows, width), F32),
        "dres": ((rows, width), F32),
        "m_all": ((2, rows, width), BF),
        "d_all": ((2, rows, width), BF),
        "pre": ((2, rows, 2 * units), F32),
        "act": ((2, rows, 2 * units), BF),
        "dpre": ((2, rows, 2 * units), BF),
        "ps": ((2, rows, width), BF),
        "pr": ((2, rows, width), BF),
        "g": ((2, 2, 2, chips, shard, units), BF),
        "gp": ((2, 2, chips, shard, units), BF),
        "gs": ((2, 2, chips, shard, units), BF),
        "gl": ((2, 2, chips, shard, units), BF),
        "zs": ((2, shard, units), BF),
        "zr": ((2, shard, units), BF),
        "a": ((2, chips, 4, shard, local), BF),
        "ap": ((chips, 4, shard, local), BF),
        "as_": ((chips, 4, shard, local), BF),
        "al": ((chips, 4, shard, local), BF),
        "sums": ((8, width), F32),
        "sp": ((8, width), F32),
        "sc": ((chips, 8, width), F32),
        "st": ((4, 8, width), F32),
        "b": ((8, local), F32),
        "bp": ((8, local), F32),
        "bc": ((chips, 8, local), F32),
    }
    semaphores = {"lsem": (12,)}
    for name, shape in {
        "m": (2,),
        "z": (5,),
        "xg": (2, n - 1, CH),
        "r1": (2, n - 1, CH),
        "w": (5, 2 * chips - 1),
        "p": (2, CH),
        "gc": (4,),
        "gx": (4, chips - 1),
        "ac": (),
        "ax": (chips - 1,),
        "sc": (chips - 1,),
        "bc": (chips - 1,),
        "st": (2,),
    }.items():
        semaphores[name + "_s"] = shape
        semaphores[name + "_r"] = shape
    names = list(operands) + list(outs) + list(buffers) + ["lengths"] + list(semaphores)

    vmem = pl.BlockSpec(memory_space=pltpu.VMEM)
    any_space = pl.BlockSpec(memory_space=pl.ANY)
    results = pl.pallas_call(
        functools.partial(layer_kernel, n, dp, names),
        out_shape=[pltpu.VMEM(shape, F32) for shape in outs.values()],
        in_specs=[any_space] * len(operands),
        out_specs=[vmem] * len(outs),
        scratch_shapes=[pltpu.VMEM(shape, kind) for shape, kind in buffers.values()]
        + [pltpu.SMEM(lengths.shape, jnp.int32)]
        + [dma(shape) if shape else dma for shape in semaphores.values()],
        compiler_params=pltpu.CompilerParams(
            collective_id=0, has_side_effects=True, vmem_limit_bytes=56 * 2**20
        ),
    )(*operands.values())
    shapes = [jax.ShapeDtypeStruct(shape, F32) for shape in outs.values()]
    hidden, dx, qkv, qvb, proj, branch, up, ub, down, gain, nb = pl.pallas_call(
        functools.partial(store_kernel, len(outs)),
        out_shape=shapes,
        in_specs=[vmem] * len(outs),
        out_specs=[any_space] * len(outs),
        scratch_shapes=[dma((len(outs),))],
    )(*[pltpu.with_memory_space_constraint(result, pltpu.VMEM) for result in results])
    return (
        hidden,
        dx,
        qkv[None],
        qvb[None],
        proj[None],
        branch[None],
        up[None],
        ub,
        down.T[None],
        gain[None],
        nb[None],
    )


def solution(mesh):
    placed = (
        P(("dp", "tensor"), None),
        P("dp"),
        P(None, None, "dp", "tensor"),
        P(None, None, "tensor"),
        P(None, "tensor", "dp"),
        P(),
        P(None, "dp", "tensor"),
        P(None, "tensor"),
        P(None, "tensor", "dp"),
        P(),
        P(),
        P(("dp", "tensor"), None),
    )
    return jax.shard_map(
        per_device,
        mesh=mesh,
        in_specs=placed,
        out_specs=(
            P(("dp", "tensor"), None),
            P(("dp", "tensor"), None),
            P(None, None, "dp", "tensor"),
            P(None, None, "tensor"),
            P(None, "tensor", "dp"),
            P(),
            P(None, "dp", "tensor"),
            P(None, "tensor"),
            P(None, "tensor", "dp"),
            P(),
            P(),
        ),
        check_vma=False,
    )
```

```python
import functools
import math
from types import SimpleNamespace

import jax
import jax.numpy as jnp
from jax import lax
from jax.experimental import pallas as pl
from jax.experimental.pallas import tpu as pltpu
from jax.sharding import PartitionSpec as P

MESH = pl.DeviceIdType.MESH
BF = jnp.bfloat16
F32 = jnp.float32
HD = 64
CH = 2

norm_eps = 1e-12
half_root = 0.7071067811865476
inv_root = 0.3989422804014327


def layer_norm(residual):
    centred = residual - jnp.mean(residual, axis=-1, keepdims=True)
    inverse = lax.rsqrt(jnp.mean(centred * centred, axis=-1, keepdims=True) + norm_eps)
    return (centred * inverse, inverse)


def norm_back(upstream, normed, inverse, gain_row):
    scaled = upstream * gain_row
    return inverse * (
        scaled
        - jnp.mean(scaled, axis=-1, keepdims=True)
        - normed * jnp.mean(scaled * normed, axis=-1, keepdims=True)
    )


def gelu_value(pre_act):
    return 0.5 * pre_act * (1.0 + lax.erf(pre_act * half_root))


def gelu_slope(pre_act):
    return (
        0.5 * (1.0 + lax.erf(pre_act * half_root))
        + pre_act * jnp.exp(-0.5 * pre_act * pre_act) * inv_root
    )


def nn_dot(left, right):
    return jnp.dot(left, right, preferred_element_type=F32)


def nt_dot(left, right):
    return lax.dot_general(left, right, (((1,), (1,)), ((), ())), preferred_element_type=F32)


def tn_dot(left, right):
    return lax.dot_general(left, right, (((0,), (0,)), ((), ())), preferred_element_type=F32)


def turned(block):
    size = block.shape[1]
    row = lax.broadcasted_iota(jnp.int32, (size, size), 0)
    col = lax.broadcasted_iota(jnp.int32, (size, size), 1)
    return nt_dot(jnp.where(row == col, 1.0, 0.0).astype(BF), block).astype(BF)


def send(src, dst, send_sem, recv_sem, axis, target):
    return pltpu.make_async_remote_copy(
        src_ref=src,
        dst_ref=dst,
        send_sem=send_sem,
        recv_sem=recv_sem,
        device_id={axis: target},
        device_id_type=MESH,
    )


def ways(me, n):
    return ((0, me, me + 1), (1, n - 1 - me, me - 1))


class ChainGather:
    def __init__(self, buf, me, n, ssem, rsem):
        self.buf, self.me, self.n, self.ssem, self.rsem = buf, me, n, ssem, rsem
        self.chunk = buf.shape[1] // CH

    def link(self, way, s, c, pos, target):
        block = pos - s
        block = block if way == 0 else self.n - 1 - block
        view = self.buf.at[block, pl.ds(c * self.chunk, self.chunk)]
        sems = self.ssem.at[way, s, c], self.rsem.at[way, s, c]
        return send(view, view, *sems, "tensor", target)

    def step(self, s, c):
        for way, pos, target in ways(self.me, self.n):

            @pl.when(jnp.logical_and(pos >= s, pos < self.n - 1))
            def _(way=way, pos=pos, target=target):
                if s > 0:
                    self.link(way, s - 1, c, pos - 1, target).wait_recv()
                self.link(way, s, c, pos, target).start()

    def steps(self, s):
        for c in range(CH):
            self.step(s, c)

    def last(self):
        for way, pos, target in ways(self.me, self.n):

            @pl.when(pos == self.n - 1)
            def _(way=way, pos=pos, target=target):
                for s in range(self.n - 1):
                    for c in range(CH):
                        self.link(way, s, c, pos - 1, target).wait_recv()

    def finish(self):
        for s in range(self.n - 1):
            for way, pos, target in ways(self.me, self.n):

                @pl.when(jnp.logical_and(pos >= s, pos < self.n - 1))
                def _(way=way, pos=pos, target=target):
                    for c in range(CH):
                        self.link(way, s, c, pos, target).wait_send()


class ChainReduce:
    def __init__(self, terms, me, n, sbuf, rbuf, ssem, rsem):
        self.terms, self.me, self.n = terms, me, n
        self.sbuf, self.rbuf, self.ssem, self.rsem = sbuf, rbuf, ssem, rsem
        self.chunk = terms.shape[1] // CH

    def part(self, c):
        return pl.ds(c * self.chunk, self.chunk)

    def link(self, way, s, c, target):
        return send(
            self.sbuf.at[way, s, self.part(c)],
            self.rbuf.at[way, s, self.part(c)],
            self.ssem.at[way, s, c],
            self.rsem.at[way, s, c],
            "tensor",
            target,
        )

    def step(self, s, c):
        for way, pos, target in ways(self.me, self.n):
            owner = self.n - 1 - s + pos
            block = owner if way == 0 else self.n - 1 - owner

            @pl.when(pos <= s)
            def _(way=way, pos=pos, target=target, block=block):
                if s == 0:
                    self.sbuf[way, s, self.part(c)] = self.terms[block, self.part(c)].astype(BF)
                else:

                    @pl.when(pos == 0)
                    def _():
                        self.link(way, s - 1, c, target).wait_send()
                        self.sbuf[way, s, self.part(c)] = self.terms[block, self.part(c)].astype(BF)

                    @pl.when(pos > 0)
                    def _():
                        self.link(way, s - 1, c, target).wait_recv()
                        got = self.rbuf[way, s - 1, self.part(c)].astype(F32)
                        self.sbuf[way, s, self.part(c)] = (
                            self.terms[block, self.part(c)] + got
                        ).astype(BF)

                self.link(way, s, c, target).start()

    def steps(self, s):
        for c in range(CH):
            self.step(s, c)

    def total(self, c, acc):
        acc[self.part(c)] = self.terms[self.me, self.part(c)]
        for way, pos, target in ways(self.me, self.n):

            @pl.when(pos > 0)
            def _(way=way, target=target):
                self.link(way, self.n - 2, c, target).wait_recv()
                acc[self.part(c)] += self.rbuf[way, self.n - 2, self.part(c)].astype(F32)

    def finish(self):
        for s in range(self.n - 1):
            for way, pos, target in ways(self.me, self.n):

                @pl.when(jnp.logical_and(pos <= s, jnp.logical_or(pos > 0, s == self.n - 2)))
                def _(way=way, target=target):
                    for c in range(CH):
                        self.link(way, s, c, target).wait_send()


class Plane:
    def __init__(self, mine, dp, way):
        chips = dp // 2
        chip = lax.div(mine, 2)
        self.core_index = lax.rem(mine, 2)
        self.mate = mine + 1 - 2 * self.core_index
        self.way = way
        if way == 0:
            self.first, self.second = chips, 1
            self.f, self.g = chip, 0
        elif way == 1:
            self.first, self.second = 2, chips // 2
            self.f, self.g = lax.rem(chip, 2), lax.div(chip, 2)
        else:
            self.first, self.second = chips // 2, 2
            self.f, self.g = lax.div(chip, 2), lax.rem(chip, 2)
        self.spots = [(i, j) for j in range(self.second) for i in range(self.first)]

    def at(self, i, j, other_core=False):
        f = lax.rem(self.f + i % self.first, self.first)
        g = lax.rem(self.g + j % self.second, self.second) if self.second > 1 else 0
        chip = f if self.way == 0 else (2 * g + f if self.way == 1 else 2 * f + g)
        return 2 * chip + (1 - self.core_index if other_core else self.core_index)

    def slot(self, i, j):
        return i * self.second + j


class PlaneGather:
    def __init__(self, buf, grid, ssem, rsem):
        self.buf, self.grid, self.ssem, self.rsem = buf, grid, ssem, rsem
        self.chips = grid.first * grid.second

    def chip(self, i, j):
        k = self.grid.slot(i, j) - 1
        sems = self.ssem.at[k], self.rsem.at[k]
        if j == 0:
            view, target = self.buf.at[self.grid.at(0, 0)], self.grid.at(i, 0)
        else:
            view, target = self.buf.at[self.grid.at(-i, 0)], self.grid.at(0, j)
        return send(view, view, *sems, "dp", target)

    def core(self, i, j):
        view = self.buf.at[self.grid.at(-i, -j)]
        k = self.chips - 1 + self.grid.slot(i, j)
        return send(view, view, self.ssem.at[k], self.rsem.at[k], "dp", self.grid.mate)

    def start(self):
        for i in range(1, self.grid.first):
            self.chip(i, 0).start()
        for j in range(1, self.grid.second):
            self.chip(0, j).start()
        self.core(0, 0).start()

    def relay(self):
        for i in range(1, self.grid.first):
            self.chip(i, 0).wait_recv()
            for j in range(1, self.grid.second):
                self.chip(i, j).start()
            self.core(i, 0).start()

    def relay_rest(self):
        for i, j in self.grid.spots:
            if j > 0:
                self.chip(i, j).wait_recv()
                self.core(i, j).start()

    def last(self):
        for i, j in self.grid.spots:
            self.core(i, j).wait_recv()

    def finish(self):
        for i, j in self.grid.spots:
            if i > 0 or j > 0:
                self.chip(i, j).wait_send()
            self.core(i, j).wait_send()


class PlaneReduce:
    def __init__(self, parts, got, summed, land, grid, sems):
        self.parts, self.got, self.summed, self.land = parts, got, summed, land
        self.grid, self.sems = grid, sems

    def core(self):
        grid = self.grid
        part = self.parts.at[1 - grid.core_index]
        return send(part, self.got, self.sems[0], self.sems[1], "dp", grid.mate)

    def chip(self, i, j):
        k = self.grid.slot(i, j)
        target = self.grid.at(-i, 0) if j == 0 else self.grid.at(0, j)
        sems = self.sems[2].at[k - 1], self.sems[3].at[k - 1]
        return send(self.summed.at[k], self.land.at[k], *sems, "dp", target)

    def start(self):
        self.core().start()

    def pair(self, i, j):
        spot = lax.div(self.grid.at(-i, j), 2)
        return self.parts[self.grid.core_index, spot].astype(F32) + self.got[spot].astype(F32)

    def spread(self):
        self.core().wait_recv()
        for i, j in reversed(self.grid.spots):
            if j > 0:
                self.summed[self.grid.slot(i, j)] = self.pair(i, j).astype(BF)
                self.chip(i, j).start()

    def row(self, i):
        total = self.pair(i, 0)
        for j in range(1, self.grid.second):
            self.chip(i, j).wait_recv()
            total = total + self.land[self.grid.slot(i, j)].astype(F32)
        return total

    def spread_rest(self):
        for i in range(1, self.grid.first):
            self.summed[self.grid.slot(i, 0)] = self.row(i).astype(BF)
            self.chip(i, 0).start()

    def total(self):
        total = self.row(0)
        for i in range(1, self.grid.first):
            self.chip(i, 0).wait_recv()
            total = total + self.land[self.grid.slot(i, 0)].astype(F32)
        return total

    def finish(self):
        self.core().wait_send()
        for i, j in self.grid.spots:
            if i > 0 or j > 0:
                self.chip(i, j).wait_send()


def joined(value):
    parts, rows, columns = value.shape
    if rows % 16 == 0:
        return value.reshape(parts * rows, columns)
    return jnp.concatenate([value[d] for d in range(parts)], axis=0)


def put_parts(ref, value, *where):
    chips, rows = ref.shape[1], ref.shape[-2]
    for d in range(2 * chips):
        ref[(d % 2, d // 2) + where] = value[d * rows : (d + 1) * rows].astype(BF)


def layer_kernel(n, dp, names, *refs):
    r = SimpleNamespace(**dict(zip(names, refs)))
    me = lax.axis_index("tensor")
    mine = lax.axis_index("dp")
    chips = dp // 2
    chip = lax.div(mine, 2)
    core_mate = mine + 1 - 2 * lax.rem(mine, 2)
    pair_mate = me + 1 - 2 * lax.rem(me, 2)
    far = lax.rem(me + n // 2, n)
    own_rows, width = r.x.shape
    local = r.q.shape[1]
    units = r.ub.shape[-1]
    chunk = own_rows // CH
    scale = 1.0 / math.sqrt(HD)

    loads = {
        name: pltpu.make_async_copy(src, dst, r.lsem.at[k])
        for k, (name, src, dst) in enumerate(
            [
                ("x", r.x_h, r.x),
                ("qkv", r.qkv_h, r.aw.at[mine, pl.ds(0, 3)]),
                ("proj", r.proj_h, r.pv),
                ("down", r.down_h, r.nd.at[mine]),
                ("up", r.up_h, r.nu.at[mine]),
                ("ub", r.ub_h, r.ub.at[0]),
                ("qvb", r.qvb_h, r.qvb),
                ("bb", r.bb_h, r.bb),
                ("gain", r.gain_h, r.gain),
                ("nb", r.nb_h, r.nb),
                ("cot", r.cot_h, r.cot),
                ("lengths", r.lengths_h, r.lengths),
            ]
        )
    }
    for copy in loads.values():
        copy.start()
    barrier = pltpu.get_barrier_semaphore()
    for k in range(1, n):
        pl.semaphore_signal(
            barrier, inc=1, device_id={"tensor": lax.rem(me + k, n)}, device_id_type=MESH
        )
    for k in range(1, chips):
        pl.semaphore_signal(
            barrier, inc=1, device_id={"dp": lax.rem(mine + 2 * k, dp)}, device_id_type=MESH
        )
    pl.semaphore_signal(barrier, inc=1, device_id={"dp": core_mate}, device_id_type=MESH)

    loads["x"].wait()
    r.xr[me] = r.x[...].astype(BF)
    loads["proj"].wait()
    r.aw[mine, 3] = turned(r.pv[...])
    for name in ("qkv", "up", "down", "ub"):
        loads[name].wait()
    pl.semaphore_wait(barrier, n - 1 + chips)

    xg = ChainGather(r.xr, me, n, r.xg_s, r.xg_r)
    grids = [Plane(mine, dp, way) for way in range(3)]
    gathers = [
        PlaneGather(buf, grids[way], r.w_s.at[k], r.w_r.at[k])
        for k, (buf, way) in enumerate(((r.aw, 0), (r.nu, 1), (r.nd, 2), (r.fu, 1), (r.fd, 2)))
    ]
    inner = jnp.logical_and(me > 0, me < n - 1)
    g_attn, g_up, g_down, g_far_up, g_far_down = gathers

    def far_copy(k):
        src, dst = (
            (r.nu.at[mine], r.fu.at[mine]),
            (r.nd.at[mine], r.fd.at[mine]),
            (r.ub.at[0], r.ub.at[1]),
            (r.zs.at[0], r.zr.at[0]),
            (r.zs.at[1], r.zr.at[1]),
        )[k]
        return send(src, dst, r.z_s.at[k], r.z_r.at[k], "tensor", far)

    def pair_copy(phase, c, src, dst):
        return send(
            src.at[pl.ds(c * chunk, chunk)],
            dst.at[pl.ds(c * chunk, chunk)],
            r.p_s.at[phase % 2, c],
            r.p_r.at[phase % 2, c],
            "tensor",
            pair_mate,
        )

    def rows_of(c):
        return pl.ds(c * chunk, chunk)

    xg.steps(0)
    g_attn.start()
    g_up.start()
    g_down.start()
    xg.steps(1)
    xg.steps(2)
    g_attn.relay()
    @pl.when(jnp.logical_not(inner))
    def _():
        for k in range(3):
            far_copy(k).start()

    for name in ("qvb", "bb", "gain", "nb", "cot", "lengths"):
        loads[name].wait()
    g_attn.last()
    xg.last()

    rounded = joined(r.xr[...])
    r.q[...] = (nn_dot(rounded, joined(r.aw[:, 0])) + r.qvb[0:1, :]).astype(BF)
    r.k[...] = nn_dot(rounded, joined(r.aw[:, 1])).astype(BF)
    r.v[...] = (nn_dot(rounded, joined(r.aw[:, 2])) + r.qvb[1:2, :]).astype(BF)
    @pl.when(inner)
    def _():
        for k in range(3):
            far_copy(k).start()

    g_up.relay()
    g_down.relay()
    seq_rows = r.q.shape[0]
    valid = lax.broadcasted_iota(jnp.int32, (seq_rows, seq_rows), 1) < r.lengths[0]
    heads = local // HD
    for head in range(heads):
        cols = slice(head * HD, (head + 1) * HD)
        scores = jnp.where(valid, nt_dot(r.q[:, cols], r.k[:, cols]) * scale, -1e30)
        weights = jnp.exp(scores - jnp.max(scores, axis=-1, keepdims=True))
        prob = weights * (1.0 / jnp.sum(weights, axis=-1, keepdims=True))
        r.prob[head] = prob
        r.ctx[:, cols] = nn_dot(prob.astype(BF), r.v[:, cols]).astype(BF)
    r.terms[...] = nt_dot(r.ctx[...], joined(r.aw[:, 3])).reshape(r.terms.shape)

    red = ChainReduce(r.terms, me, n, r.s1, r.r1, r.r1_s, r.r1_r)
    red.steps(0)
    far_copy(0).wait_recv()
    g_far_up.start()
    red.steps(1)
    far_copy(1).wait_recv()
    g_far_down.start()
    g_up.relay_rest()
    g_down.relay_rest()
    red.steps(2)
    g_far_up.relay()
    g_far_down.relay()
    g_up.last()
    g_down.last()
    r.dt[...] = joined(r.nd[...]).T
    r.ut[0] = joined(r.nu[...]).T
    for c in range(CH):
        part = rows_of(c)
        red.total(c, r.acc)
        normed, inverse = layer_norm(r.x[part] + r.acc[part] + r.bb[0:1, :])
        middle = normed * r.gain[0:1, :] + r.nb[0:1, :]
        r.n1[part] = normed
        r.i1[part] = inverse
        r.mid[part] = middle
        r.m_all[0, part] = middle.astype(BF)
        pair_copy(0, c, r.m_all.at[0], r.m_all.at[1]).start()
    g_far_up.relay_rest()
    far_copy(2).wait_recv()

    def up_of(h):
        return r.nu[...] if h == 0 else r.fu[...]

    def down_of(h):
        return r.nd[...] if h == 0 else r.fd[...]

    every = slice(0, own_rows)
    halves = [slice(c * chunk, (c + 1) * chunk) for c in range(CH)]

    def up_rows(group, h, part):
        cols = slice(h * units, (h + 1) * units)
        pre = nn_dot(r.m_all[group, part], joined(up_of(h))) + r.ub[h]
        r.pre[group, part, cols] = pre
        r.act[group, part, cols] = gelu_value(pre).astype(BF)

    def down_rows(group, part):
        return nn_dot(r.act[group, part, :units], r.dt[...]) + nt_dot(
            r.act[group, part, units:], joined(down_of(1))
        )

    up_rows(0, 0, every)
    for c, part in enumerate(halves):
        pair_copy(0, c, r.m_all.at[0], r.m_all.at[1]).wait_recv()
        up_rows(1, 0, part)
        if c == 0:
            g_far_up.last()
        up_rows(1, 1, part)
        if c == 0:
            g_far_down.relay_rest()
            g_far_down.last()
        r.ps[0, part] = down_rows(1, part).astype(BF)
        pair_copy(1, c, r.ps.at[0], r.pr.at[0]).start()
    up_rows(0, 1, every)
    r.acc[...] = down_rows(0, every)
    for group in range(2):
        for h in range(2):
            cols = slice(h * units, (h + 1) * units)
            r.pre[group, :, cols] = gelu_slope(r.pre[group, :, cols])

    r.ut[1] = joined(up_of(1)).T
    for c in range(CH):
        part = rows_of(c)
        pair_copy(1, c, r.ps.at[0], r.pr.at[0]).wait_recv()
        normed, inverse = layer_norm(
            r.mid[part] + r.acc[part] + r.pr[0, part].astype(F32) + r.bb[1:2, :]
        )
        dres = norm_back(r.cot[part], normed, inverse, r.gain[1:2, :])
        r.d_all[0, part] = dres.astype(BF)
        pair_copy(0, c, r.m_all.at[0], r.m_all.at[1]).wait_send()
        pair_copy(2, c, r.d_all.at[0], r.d_all.at[1]).start()
        r.dres[part] = dres
        r.acc[part] = normed
    r.hidden_o[...] = r.acc[...] * r.gain[1:2, :] + r.nb[1:2, :]
    r.sums[3:4, :] = jnp.sum(r.cot[...] * r.acc[...], axis=0, keepdims=True)
    r.sums[4:5, :] = jnp.sum(r.cot[...], axis=0, keepdims=True)
    r.sums[5:6, :] = jnp.sum(r.dres[...], axis=0, keepdims=True)

    def back_rows(group, h, part):
        cols = slice(h * units, (h + 1) * units)
        dpre = nn_dot(r.d_all[group, part], joined(down_of(h))) * r.pre[group, part, cols]
        r.dpre[group, part, cols] = dpre.astype(BF)
        total = jnp.sum(dpre, axis=0, keepdims=True)
        r.sums[6 + h : 7 + h, :] = total if group == 0 else r.sums[6 + h : 7 + h, :] + total

    def up_back(group, part):
        return nn_dot(r.dpre[group, part, :units], r.ut[0]) + nn_dot(
            r.dpre[group, part, units:], r.ut[1]
        )

    back_rows(0, 0, every)
    back_rows(0, 1, every)
    for c, part in enumerate(halves):
        pair_copy(2, c, r.d_all.at[0], r.d_all.at[1]).wait_recv()
        back_rows(1, 0, part)
        back_rows(1, 1, part)
        r.ps[1, part] = up_back(1, part).astype(BF)
        pair_copy(1, c, r.ps.at[0], r.pr.at[0]).wait_send()
        pair_copy(3, c, r.ps.at[1], r.pr.at[1]).start()
    xg.finish()
    red.finish()
    reduces = {
        (h, t): PlaneReduce(
            r.g.at[h, t], r.gp.at[h, t], r.gs.at[h, t], r.gl.at[h, t], grids[0 if h else 1 + t],
            [sem.at[2 * h + t] for sem in (r.gc_s, r.gc_r, r.gx_s, r.gx_r)],
        )
        for h in range(2)
        for t in range(2)
    }

    def weight_part(h, t):
        cols = slice(h * units, (h + 1) * units)
        if t == 0:
            left, right = r.m_all[...], r.dpre[:, :, cols]
        else:
            left, right = r.d_all[...], r.act[:, :, cols]
        put_parts(r.g.at[h, t], tn_dot(joined(left), joined(right)))
        reduces[h, t].start()

    weight_part(1, 1)
    weight_part(1, 0)
    r.acc[...] = up_back(0, every) + r.dres[...]
    reduces[1, 1].spread()
    reduces[1, 1].spread_rest()
    weight_part(0, 1)
    weight_part(0, 0)
    dg = ChainGather(r.dr, me, n, r.xg_s, r.xg_r)
    for c in range(CH):
        part = rows_of(c)
        pair_copy(3, c, r.ps.at[1], r.pr.at[1]).wait_recv()
        dmid = r.acc[part] + r.pr[1, part].astype(F32)
        dres = norm_back(dmid, r.n1[part], r.i1[part], r.gain[0:1, :])
        r.dr[me, part] = dres.astype(BF)
        dg.step(0, c)
        r.acc[part] = dmid
        r.dres[part] = dres
    reduces[1, 0].spread()
    reduces[1, 0].spread_rest()
    r.sums[0:1, :] = jnp.sum(r.acc[...] * r.n1[...], axis=0, keepdims=True)
    r.sums[1:2, :] = jnp.sum(r.acc[...], axis=0, keepdims=True)
    r.sums[2:3, :] = jnp.sum(r.dres[...], axis=0, keepdims=True)

    def sum_mate():
        return send(r.sums, r.sp, r.m_s.at[0], r.m_r.at[0], "dp", core_mate)

    def bias_mate():
        return send(r.b, r.bp, r.m_s.at[1], r.m_r.at[1], "dp", core_mate)

    def bias_chip(k):
        view = r.bc.at[chip]
        sems = r.bc_s.at[k - 1], r.bc_r.at[k - 1]
        return send(view, view, *sems, "dp", lax.rem(mine + 2 * k, dp))

    def sum_chip(k):
        view = r.sc.at[chip]
        sems = r.sc_s.at[k - 1], r.sc_r.at[k - 1]
        return send(view, view, *sems, "dp", lax.rem(mine + 2 * k, dp))

    def sum_pair():
        return send(r.st.at[0], r.st.at[1], r.st_s.at[0], r.st_r.at[0], "tensor", pair_mate)

    def sum_far():
        return send(r.st.at[2], r.st.at[3], r.st_s.at[1], r.st_r.at[1], "tensor", far)

    sum_mate().start()
    dg.steps(1)
    sum_mate().wait_recv()
    r.sc[chip] = r.sums[...] + r.sp[...]
    for k in range(1, chips):
        sum_chip(k).start()
    dg.steps(2)
    def far_total(t):
        r.zs[t] = reduces[1, t].total().astype(BF)

    far_total(1)

    @pl.when(jnp.logical_not(inner))
    def _():
        far_copy(4).start()
        far_total(0)
        far_copy(3).start()

    reduces[0, 1].spread()
    reduces[0, 0].spread()
    dg.last()

    for k in range(1, chips):
        sum_chip(k).wait_recv()
    total = r.sc[0]
    for k in range(1, chips):
        total = total + r.sc[k]
    r.st[0] = total
    sum_pair().start()
    @pl.when(inner)
    def _():
        far_copy(4).start()

    dres_all = joined(r.dr[...])
    r.dctx[...] = nn_dot(dres_all, joined(r.aw[:, 3])).astype(BF)
    r.b[...] = jnp.zeros_like(r.b)
    for head in range(heads):
        cols = slice(head * HD, (head + 1) * HD)
        prob = r.prob[head]
        dc = r.dctx[:, cols]
        dprob = nt_dot(dc, r.v[:, cols])
        weighted = jnp.sum(prob * dprob, axis=-1, keepdims=True)
        dscore = (prob * (dprob - weighted) * scale).astype(BF)
        dquery = nn_dot(dscore, r.k[:, cols])
        dvalue = tn_dot(prob.astype(BF), dc)
        r.dm[0, :, cols] = dquery.astype(BF)
        r.dm[1, :, cols] = tn_dot(dscore, r.q[:, cols]).astype(BF)
        r.dm[2, :, cols] = dvalue.astype(BF)
        r.b[0:1, cols] = jnp.sum(dquery, axis=0, keepdims=True)
        r.b[1:2, cols] = jnp.sum(dvalue, axis=0, keepdims=True)
    bias_mate().start()
    dx = nt_dot(r.dm[0], joined(r.aw[:, 0]))
    for j in range(1, 3):
        dx = dx + nt_dot(r.dm[j], joined(r.aw[:, j]))
    r.terms[...] = dx.reshape(r.terms.shape)

    red_x = ChainReduce(r.terms, me, n, r.s2, r.r2, r.r1_s, r.r1_r)
    red_x.steps(0)
    @pl.when(inner)
    def _():
        far_total(0)
        far_copy(3).start()

    bias_mate().wait_recv()
    r.bc[chip] = r.b[...] + r.bp[...]
    for k in range(1, chips):
        bias_chip(k).start()
    sum_pair().wait_recv()
    r.st[2, 0:6] = r.st[0, 0:6] + r.st[1, 0:6]
    r.st[2, 6:8] = r.st[0, 6:8]
    sum_far().start()
    reduces[0, 1].spread_rest()
    reduces[0, 0].spread_rest()
    attn = PlaneReduce(
        r.a, r.ap, r.as_, r.al, grids[0], (r.ac_s, r.ac_r, r.ax_s, r.ax_r)
    )
    rounded = joined(r.xr[...])
    for j in range(3):
        put_parts(r.a, tn_dot(rounded, r.dm[j]), j)
    put_parts(r.a, tn_dot(joined(r.dr[...]), r.ctx[...]), 3)
    attn.start()
    red_x.steps(1)
    attn.spread()
    attn.spread_rest()
    red_x.steps(2)

    sum_far().wait_recv()
    total = r.st[2] + r.st[3]
    for j in range(2):
        for k, ref in enumerate((r.gain_o, r.nb_o, r.branch_o)):
            ref[j : j + 1, :] = total[3 * j + k : 3 * j + k + 1]
    r.ub_o[...] = r.st[0, 6:7] + r.st[3, 7:8]
    for k in range(1, chips):
        bias_chip(k).wait_recv()
    total = r.bc[0]
    for k in range(1, chips):
        total = total + r.bc[k]
    r.qvb_o[...] = total[0:2]
    for c in range(CH):
        red_x.total(c, r.acc)
    r.dx_o[...] = r.acc[...] + r.dres[...]
    for t, out in enumerate((r.up_o, r.down_o)):
        out[...] = reduces[0, t].total()
    for t, out in ((1, r.down_o), (0, r.up_o)):
        far_copy(3 + t).wait_recv()
        out[...] += r.zr[t].astype(F32)
    total = attn.total()
    r.qkv_o[...] = total[0:3]
    r.proj_o[...] = total[3].T

    dg.finish()
    red_x.finish()
    for gather in gathers:
        gather.finish()
    for reduce in list(reduces.values()) + [attn]:
        reduce.finish()
    for k in range(5):
        far_copy(k).wait_send()
    for c in range(CH):
        pair_copy(2, c, r.d_all.at[0], r.d_all.at[1]).wait_send()
        pair_copy(3, c, r.ps.at[1], r.pr.at[1]).wait_send()
    sum_mate().wait_send()
    bias_mate().wait_send()
    for k in range(1, chips):
        sum_chip(k).wait_send()
        bias_chip(k).wait_send()
    sum_pair().wait_send()
    sum_far().wait_send()


def store_kernel(count, *refs):
    sems = refs[2 * count]
    copies = [
        pltpu.make_async_copy(refs[k], refs[count + k], sems.at[k]) for k in range(count)
    ]
    for copy in copies:
        copy.start()
    for copy in copies:
        copy.wait()


def per_device(
    inputs,
    lengths,
    qkv_weight,
    qv_bias,
    proj_weight,
    branch_bias,
    up_weight,
    up_bias,
    down_weight,
    norm_gain,
    norm_bias,
    cotangent,
):
    n = lax.axis_size("tensor")
    dp = lax.axis_size("dp")
    rows, width = inputs.shape
    shard, local = qkv_weight.shape[2:]
    units = up_weight.shape[2]
    chips = dp // 2
    seq = rows * n
    heads = local // HD
    dma = pltpu.SemaphoreType.DMA

    operands = {
        "lengths_h": lengths,
        "x_h": inputs,
        "qkv_h": qkv_weight[0],
        "qvb_h": qv_bias[0],
        "proj_h": proj_weight[0],
        "bb_h": branch_bias[0],
        "up_h": up_weight[0],
        "ub_h": up_bias,
        "down_h": down_weight[0].T,
        "gain_h": norm_gain[0],
        "nb_h": norm_bias[0],
        "cot_h": cotangent,
    }
    outs = {
        "hidden_o": (rows, width),
        "dx_o": (rows, width),
        "qkv_o": (3, shard, local),
        "qvb_o": (2, local),
        "proj_o": (local, shard),
        "branch_o": (2, width),
        "up_o": (shard, units),
        "ub_o": (1, units),
        "down_o": (shard, units),
        "gain_o": (2, width),
        "nb_o": (2, width),
    }
    chain = (2, n - 1, rows, width)
    buffers = {
        "x": ((rows, width), F32),
        "cot": ((rows, width), F32),
        "xr": ((n, rows, width), BF),
        "dr": ((n, rows, width), BF),
        "aw": ((dp, 4, shard, local), BF),
        "pv": ((local, shard), BF),
        "nu": ((dp, shard, units), BF),
        "nd": ((dp, shard, units), BF),
        "dt": ((units, width), BF),
        "ut": ((2, units, width), BF),
        "fu": ((dp, shard, units), BF),
        "fd": ((dp, shard, units), BF),
        "qvb": ((2, local), F32),
        "bb": ((2, width), F32),
        "ub": ((2, 1, units), F32),
        "gain": ((2, width), F32),
        "nb": ((2, width), F32),
        "q": ((seq, local), BF),
        "k": ((seq, local), BF),
        "v": ((seq, local), BF),
        "ctx": ((seq, local), BF),
        "dctx": ((seq, local), BF),
        "dm": ((3, seq, local), BF),
        "prob": ((heads, seq, seq), F32),
        "terms": ((n, rows, width), F32),
        "s1": (chain, BF),
        "r1": (chain, BF),
        "s2": (chain, BF),
        "r2": (chain, BF),
        "acc": ((rows, width), F32),
        "n1": ((rows, width), F32),
        "i1": ((rows, 1), F32),
        "mid": ((rows, width), F32),
        "dres": ((rows, width), F32),
        "m_all": ((2, rows, width), BF),
        "d_all": ((2, rows, width), BF),
        "pre": ((2, rows, 2 * units), F32),
        "act": ((2, rows, 2 * units), BF),
        "dpre": ((2, rows, 2 * units), BF),
        "ps": ((2, rows, width), BF),
        "pr": ((2, rows, width), BF),
        "g": ((2, 2, 2, chips, shard, units), BF),
        "gp": ((2, 2, chips, shard, units), BF),
        "gs": ((2, 2, chips, shard, units), BF),
        "gl": ((2, 2, chips, shard, units), BF),
        "zs": ((2, shard, units), BF),
        "zr": ((2, shard, units), BF),
        "a": ((2, chips, 4, shard, local), BF),
        "ap": ((chips, 4, shard, local), BF),
        "as_": ((chips, 4, shard, local), BF),
        "al": ((chips, 4, shard, local), BF),
        "sums": ((8, width), F32),
        "sp": ((8, width), F32),
        "sc": ((chips, 8, width), F32),
        "st": ((4, 8, width), F32),
        "b": ((8, local), F32),
        "bp": ((8, local), F32),
        "bc": ((chips, 8, local), F32),
    }
    semaphores = {"lsem": (12,)}
    for name, shape in {
        "m": (2,),
        "z": (5,),
        "xg": (2, n - 1, CH),
        "r1": (2, n - 1, CH),
        "w": (5, 2 * chips - 1),
        "p": (2, CH),
        "gc": (4,),
        "gx": (4, chips - 1),
        "ac": (),
        "ax": (chips - 1,),
        "sc": (chips - 1,),
        "bc": (chips - 1,),
        "st": (2,),
    }.items():
        semaphores[name + "_s"] = shape
        semaphores[name + "_r"] = shape
    names = list(operands) + list(outs) + list(buffers) + ["lengths"] + list(semaphores)

    vmem = pl.BlockSpec(memory_space=pltpu.VMEM)
    any_space = pl.BlockSpec(memory_space=pl.ANY)
    results = pl.pallas_call(
        functools.partial(layer_kernel, n, dp, names),
        out_shape=[pltpu.VMEM(shape, F32) for shape in outs.values()],
        in_specs=[any_space] * len(operands),
        out_specs=[vmem] * len(outs),
        scratch_shapes=[pltpu.VMEM(shape, kind) for shape, kind in buffers.values()]
        + [pltpu.SMEM(lengths.shape, jnp.int32)]
        + [dma(shape) if shape else dma for shape in semaphores.values()],
        compiler_params=pltpu.CompilerParams(
            collective_id=0, has_side_effects=True, vmem_limit_bytes=56 * 2**20
        ),
    )(*operands.values())
    shapes = [jax.ShapeDtypeStruct(shape, F32) for shape in outs.values()]
    hidden, dx, qkv, qvb, proj, branch, up, ub, down, gain, nb = pl.pallas_call(
        functools.partial(store_kernel, len(outs)),
        out_shape=shapes,
        in_specs=[vmem] * len(outs),
        out_specs=[any_space] * len(outs),
        scratch_shapes=[dma((len(outs),))],
    )(*[pltpu.with_memory_space_constraint(result, pltpu.VMEM) for result in results])
    return (
        hidden,
        dx,
        qkv[None],
        qvb[None],
        proj[None],
        branch[None],
        up[None],
        ub,
        down.T[None],
        gain[None],
        nb[None],
    )


def solution(mesh):
    placed = (
        P(("dp", "tensor"), None),
        P("dp"),
        P(None, None, "dp", "tensor"),
        P(None, None, "tensor"),
        P(None, "tensor", "dp"),
        P(),
        P(None, "dp", "tensor"),
        P(None, "tensor"),
        P(None, "tensor", "dp"),
        P(),
        P(),
        P(("dp", "tensor"), None),
    )
    return jax.shard_map(
        per_device,
        mesh=mesh,
        in_specs=placed,
        out_specs=(
            P(("dp", "tensor"), None),
            P(("dp", "tensor"), None),
            P(None, None, "dp", "tensor"),
            P(None, None, "tensor"),
            P(None, "tensor", "dp"),
            P(),
            P(None, "dp", "tensor"),
            P(None, "tensor"),
            P(None, "tensor", "dp"),
            P(),
            P(),
        ),
        check_vma=False,
    )
```
